256 devices in a mesh: gx: 8 (over y, core), gy: 32 (over x, z).
Axes of the slice: x: 4, y: 4, z: 8, core: 2. Of those that a mesh axis runs over, the one named last changes fastest.
Arguments:
- control: float32 [1, 2, 6, 1536, 3072], P(None, None, None, 'gy', 'gx'), may hold values from -6 to 6
- sigma: float32 [2, 6, 1536, 3072], P(None, None, 'gy', 'gx'), may hold values from 0.5 to 5
- kappa: float32 [5, 1536, 3072], P(None, 'gy', 'gx'), may hold values from 0.05 to 5
- beta: float32 [6, 1536, 3072], P(None, 'gy', 'gx'), may hold values from -3 to 3
- sea_mask: int32 [1536, 3072], P('gy', 'gx'), may hold values 0 or 1
- x_inverse: float32 [3072, 3072], P('gx'), as said below
- y_inverse: float32 [1536, 1536], P('gx')
- ssh_coef: float32 [2, 6], replicated, may hold values from -1.5 to 1.5
- obs_owner: int32 [65536, 1], P(('gx', 'gy')), may hold values from 0 to 255; in each aligned block of 256 rows (0 to 255, 256 to 511, ...) at most 2 rows name the same one
- tile_index: int32 [65536], P(('gx', 'gy')), may hold values from 0 to 18046, as said below
- obs_frac: float32 [2, 65536], P(None, ('gx', 'gy')), may hold values from 0 to 1
- obs_count: int32 [256], P(('gx', 'gy')), may hold values from 128 to 256
Outputs:
- increments: float32 [1, 2, 6, 1536, 3072], P(None, None, None, 'gy', 'gx')
- sea_height: float32 [1, 1536, 3072], P(None, 'gy', 'gx')
- obs_equiv: float32 [2, 13, 65536], P(None, None, ('gx', 'gy'))
The draws below stay inside these ranges and needn't reach their ends.
Inputs may be any that keep to these rules, and one draw needn't show every extreme that they name: `obs_owner`: among the slots of one device, at most 2 name the same owner. `tile_index`: row * 384 + column of a cell in the device's own tile, with row below 47 and column below 383. `x_inverse`: the zonal inverse is symmetric.
All inputs are finite; a program needn't handle non-finite values. No bound on the sum of `sea_mask` on one device may be relied on, other than what follows from the above.
Results may differ from the reference program's by a relative error of at most 0.00013.
Values sent between devices are 32-bit elements; how exact they have to be, the bound alone decides.
A program may use at most 128 MiB of HBM per device.

```python
import math
import jax
import jax.numpy as jnp
import numpy as np
from jax import lax

VECS = 1
LEV = 6
LAT_DEV = 48
LON_DEV = 384
STEPS = 2
CAP = 2
NY = 1536
NX = 3072
OBS_DEV = 256
REC = 13
N_GY = 32
DEVICES = 256


def draw_x_inverse(key, part):
    first_key, second_key = jax.random.split(jax.random.fold_in(key, 11))
    row_ids = jnp.arange(NX)[:, None]
    col_ids = jnp.arange(NX)[None, :]
    gap = jnp.abs(row_ids - col_ids)
    gap = jnp.minimum(gap, NX - gap).astype(jnp.float32)
    reach = 2.0 * LON_DEV
    rough = jax.random.uniform(first_key, (NX, NX), jnp.float32)
    rough = 0.5 * (rough + rough.T)
    spread = rough * jnp.exp(-gap / reach) * (0.5 / reach)
    diagonal = jax.random.uniform(second_key, (NX, 1), jnp.float32, 0.5, 1.0)
    return jnp.where(row_ids == col_ids, diagonal, spread).astype(jnp.float32)


def draw_y_inverse(key, part):
    first_key, second_key = jax.random.split(jax.random.fold_in(key, 23))
    row_ids = jnp.arange(NY)[:, None]
    col_ids = jnp.arange(NY)[None, :]
    gap = jnp.abs(row_ids - col_ids).astype(jnp.float32)
    reach = 2.0 * LAT_DEV
    rough = jax.random.uniform(first_key, (NY, NY), jnp.float32)
    spread = rough * jnp.exp(-gap / reach) * (0.5 / reach)
    diagonal = jax.random.uniform(second_key, (NY, 1), jnp.float32, 0.5, 1.0)
    return jnp.where(row_ids == col_ids, diagonal, spread).astype(jnp.float32)


def draw_tile_index(key, part):
    first_key, second_key = jax.random.split(jax.random.fold_in(key, 37))
    row_pick = jax.random.randint(first_key, (DEVICES * OBS_DEV,), 0, LAT_DEV - 1)
    col_pick = jax.random.randint(second_key, (DEVICES * OBS_DEV,), 0, LON_DEV - 1)
    picked = (row_pick * LON_DEV + col_pick).astype(jnp.int32)
    picked = picked.at[0].set(jnp.int32((LAT_DEV - 1) * LON_DEV - 2))
    picked = picked.at[1].set(jnp.int32(0))
    return picked.astype(jnp.int32)


def touch_ends(values, key, least, top_value):
    longest = values.shape.index(max(values.shape))
    spots = []
    for shift in (0, 1):
        where = [jax.random.randint(jax.random.fold_in(key, axis), (), 0, length) for axis, length in enumerate(values.shape)]
        where[longest] = (where[longest] + shift) % values.shape[longest]
        spots.append(tuple(where))
    return values.at[spots[0]].set(least).at[spots[1]].set(top_value)


def block_levels(key, dims, cuts, least, high):
    def one(dim, shards_of):
        steps = jax.random.uniform(jax.random.fold_in(jax.random.fold_in(key, 6), dim), (shards_of,), jnp.float32, least / len(cuts), high / len(cuts))
        return jnp.repeat(jnp.exp(steps), dims[dim] // shards_of).reshape((-1,) + (1,) * (len(dims) - dim - 1))

    gain = one(*cuts[0])
    for cut in cuts[1:]:
        gain = gain * one(*cut)
    return gain


def assign_block(rng, own, number, rows, amount, top, limit, lean):
    sequence = jax.random.permutation(rng, amount)
    heavy_load, usual = shares(amount, rows * top, limit, lean, True), shares(amount, rows * top, limit, lean, False)
    places = jnp.arange(amount)

    def named(tallies, rotation):
        used = int((tallies > 0).sum())
        fixed = max(1, used // 4)
        passed = fixed + (places - fixed + rotation * (used - fixed)) % max(1, amount - fixed)
        return jnp.zeros((amount,), jnp.int32).at[sequence[jnp.where(places < fixed, places, passed)]].set(jnp.asarray(tallies, jnp.int32))

    tallies = jnp.where(number % 4 == 0, named(heavy_load, number // 4), named(usual, number - number // 4 - 1))
    mixed = jax.random.permutation(jax.random.fold_in(own, 3), amount)
    donor, taker = mixed[0:amount // 2 * 2:2], mixed[1:amount // 2 * 2:2]
    margin = jnp.minimum(tallies[donor] - 1, limit - tallies[taker]) // 2
    margin = jnp.where((donor == sequence[0]) | (taker == sequence[0]) | (tallies[taker] == 0), 0, jnp.maximum(margin, 0))
    passed = jax.random.randint(jax.random.fold_in(own, 4), (amount // 2,), 0, 1 << 20) % (margin + 1)
    tallies = tallies.at[donor].add(-passed).at[taker].add(passed)
    labels = jnp.searchsorted(jnp.cumsum(tallies), jnp.arange(rows * top), side="right").astype(jnp.int32)
    listing = labels.reshape(top, rows).T
    listing = listing[jax.random.permutation(jax.random.fold_in(own, 1), rows)]
    rotation = jax.random.randint(jax.random.fold_in(own, 2), (rows, 1), 0, top)
    return jnp.take_along_axis(listing, (jnp.arange(top)[None, :] + rotation) % top, axis=1)


def shares(count, total, limit, lean, full):
    loads = [(1 << 20) // math.isqrt(rank ** lean) + 1 for rank in range(1, count + 1)]
    largest = limit if full else min(limit, max(-(-total // count), total * loads[0] // sum(loads)))
    least = 1 if total - largest >= count - 1 else 0
    given, spare = [largest] + [least] * (count - 1), total - largest - least * (count - 1)
    while spare > 0:
        candidates = [i for i in range(1, count) if given[i] < largest] or [i for i in range(1, count) if given[i] < limit]
        whole, remaining = sum([loads[i] for i in candidates]), spare
        for i in candidates:
            extra = min(limit - given[i], max(1, remaining * loads[i] // whole), spare)
            given[i] = given[i] + extra
            spare = spare - extra
    return np.array(given)


def centred(rng, shape, scale, most, cuts=(), kind=jnp.bfloat16):
    drawn = jax.random.normal(rng, shape, jnp.float32) * scale
    if len(cuts) > 0:
        drawn = block_levels(rng, shape, cuts, -0.22, 0.18) * drawn
    return jnp.clip(drawn, min=-most, max=most).astype(kind)


def setup_inputs(seed: int = 0) -> dict:
    key_list = jax.random.split(jax.random.key(seed), 13)
    control = centred(key_list[0], (VECS, 2, LEV, NY, NX), 1.0, 6.0, ((3, 32), (4, 8)), jnp.float32)
    sigma = jnp.clip(jnp.exp(math.log(5.0) - 2.3025851 * jax.random.uniform(key_list[1], (2, LEV, NY, NX), jnp.float32) ** block_levels(key_list[1], (2, LEV, NY, NX), ((2, 32), (3, 8)), -0.2, 0.2)), 0.5, 5.0)
    kappa = jnp.clip(jnp.exp(math.log(5.0) - 4.6051702 * jax.random.uniform(key_list[2], (LEV - 1, NY, NX), jnp.float32) ** block_levels(key_list[2], (LEV - 1, NY, NX), ((1, 32), (2, 8)), -0.2, 0.2)), 0.05, 5.0)
    beta = centred(key_list[3], (LEV, NY, NX), 0.5, 3.0, ((1, 32), (2, 8)), jnp.float32)
    sea_mask = touch_ends((jax.random.randint(key_list[4], (NY, NX), 0, 5) < 4).astype(jnp.int32), jax.random.fold_in(key_list[4], 1), 0, 1)
    x_inverse = draw_x_inverse(jax.random.fold_in(key_list[12], 71), 0)
    y_inverse = draw_y_inverse(jax.random.fold_in(key_list[12], 71), 0)
    ssh_coef = centred(key_list[7], (2, LEV), 0.3, 1.5, (), jnp.float32)
    obs_owner_keys = jax.random.split(jax.random.fold_in(key_list[8], 1), (DEVICES * OBS_DEV) // OBS_DEV)
    obs_owner_turns = jax.random.permutation(jax.random.fold_in(key_list[8], 3), (DEVICES * OBS_DEV) // OBS_DEV)
    obs_owner = jax.vmap(lambda own, number: assign_block(jax.random.fold_in(key_list[8], 2), own, number, OBS_DEV, DEVICES, 1, CAP, 2))(obs_owner_keys, obs_owner_turns).reshape((DEVICES * OBS_DEV, 1))
    tile_index = draw_tile_index(jax.random.fold_in(key_list[12], 71), 0)
    obs_frac = jnp.clip(1.0 * jax.random.uniform(key_list[10], (2, DEVICES * OBS_DEV), jnp.float32) ** block_levels(key_list[10], (2, DEVICES * OBS_DEV), ((1, 256),), -0.2, 0.2), 0.0, 1.0)
    obs_count = touch_ends(jax.random.randint(key_list[11], (DEVICES,), OBS_DEV // 2, OBS_DEV + 1), jax.random.fold_in(key_list[11], 1), OBS_DEV // 2, OBS_DEV).astype(jnp.int32)
    return dict(control=control, sigma=sigma, kappa=kappa, beta=beta, sea_mask=sea_mask, x_inverse=x_inverse, y_inverse=y_inverse, ssh_coef=ssh_coef, obs_owner=obs_owner, tile_index=tile_index, obs_frac=obs_frac, obs_count=obs_count)


def vertical(values, kappa):
    levels = values.shape[2]
    c_list = []
    d_list = []
    for level in range(levels):
        k_below = kappa[level - 1] if level > 0 else 0.0
        k_above = kappa[level] if level < levels - 1 else 0.0
        diag_term = 1.0 + k_below + k_above
        if level == 0:
            pivot = diag_term
            d_new = values[:, :, 0] / pivot
        else:
            pivot = diag_term + k_below * c_list[-1]
            d_new = (values[:, :, level] + k_below * d_list[-1]) / pivot
        c_list.append(-k_above / pivot)
        d_list.append(d_new)
    result = [d_list[-1]]
    for level in range(levels - 2, -1, -1):
        result.insert(0, d_list[level] - c_list[level] * result[0])
    return jnp.stack(result, axis=2)


def reference(control, sigma, kappa, beta, sea_mask, x_inverse, y_inverse, ssh_coef, obs_owner, tile_index, obs_frac, obs_count):
    highest = lax.Precision.HIGHEST
    sea_open = sea_mask.astype(jnp.float32)
    grid_field = control.reshape(VECS * 2 * LEV, NY, NX)
    for diffusion_step in range(STEPS):
        grid_field = sea_open * jnp.einsum('fyb,ab->fya', grid_field, x_inverse, precision=highest)
        grid_field = sea_open * jnp.einsum('ab,fbx->fax', y_inverse, grid_field, precision=highest)
        grid_field = vertical(grid_field.reshape(VECS, 2, LEV, NY, NX), kappa).reshape(VECS * 2 * LEV, NY, NX)
    grid_field = grid_field.reshape(VECS, 2, LEV, NY, NX)
    temper = sigma[0] * grid_field[:, 0]
    saline = sigma[1] * grid_field[:, 1] + beta * temper
    height = jnp.sum(ssh_coef[0][None, :, None, None] * temper + ssh_coef[1][None, :, None, None] * saline, axis=1)
    increments = jnp.stack([temper, saline], axis=1)
    profile = jnp.concatenate([temper, saline, height[:, None]], axis=1)
    every = jnp.arange(DEVICES * OBS_DEV, dtype=jnp.int32)
    source = every // OBS_DEV
    slot_index = every % OBS_DEV
    col_block = source // N_GY
    row_block = source % N_GY
    row_index = row_block * LAT_DEV + tile_index // LON_DEV
    col_index = col_block * LON_DEV + tile_index % LON_DEV
    frac_x = obs_frac[0]
    frac_y = obs_frac[1]
    corner_a = profile[:, :, row_index, col_index]
    corner_b = profile[:, :, row_index, col_index + 1]
    corner_c = profile[:, :, row_index + 1, col_index]
    corner_d = profile[:, :, row_index + 1, col_index + 1]
    interp = (1.0 - frac_y) * ((1.0 - frac_x) * corner_a + frac_x * corner_b) + frac_y * ((1.0 - frac_x) * corner_c + frac_x * corner_d)
    live_slot = (slot_index < obs_count[source]).astype(jnp.float32)
    interp = (interp * live_slot).reshape(REC, DEVICES * OBS_DEV)
    owners = obs_owner[:, 0]
    per_device = owners.reshape(DEVICES, OBS_DEV)
    one_hot = (per_device[:, :, None] == jnp.arange(DEVICES, dtype=jnp.int32)[None, None, :]).astype(jnp.int32)
    before = jnp.cumsum(one_hot, axis=1) - one_hot
    slot_rank = jnp.sum(before * one_hot, axis=2).reshape(-1).astype(jnp.int32)
    target = (owners * DEVICES + source).astype(jnp.int32)
    obs_equiv = jnp.zeros((CAP, REC, DEVICES * DEVICES), jnp.float32).at[slot_rank, :, target].set(interp.T)
    return increments, height, obs_equiv
```

```python
import functools

import jax
import jax.numpy as jnp
from jax import lax
from jax.experimental import pallas as pl
from jax.experimental.pallas import tpu as pltpu
from jax.sharding import PartitionSpec as P

F32, BF16, I32 = jnp.float32, jnp.bfloat16, jnp.int32
MESH = pl.DeviceIdType.MESH
ANY = pl.ANY

STEPS, KINDS, LEV = 2, 2, 6
ROWS, COLS, LANES = 48, 384, 128
LB = COLS // LANES
UNITS = LEV * LB
YR, NX, NZ = 4, 4, 8
GX, GY = 2 * YR, NX * NZ
NLAT, NLON = GY * ROWS, GX * COLS
YSH = NLAT // GX
YSB = YSH // NX
SLOTS, CAP, REC, DEV = 256, 2, 13, GX * GY
HALF = LEV // 2


def split2(v):
    hi = v.astype(BF16)
    lo = (v - hi.astype(F32)).astype(BF16)
    return hi, lo


def kernel(
    ctrl,
    sigma,
    kappa,
    beta,
    sea,
    xinv,
    yinv,
    ssh,
    owner,
    tidx,
    frac,
    count,
    inc,
    height,
    obs,
    G,
    XT,
    xbuf,
    Yf,
    Yhi,
    Ylo,
    U,
    R,
    xout,
    yout,
    F,
    acc,
    W,
    cs,
    rp,
    sig_v,
    kap_v,
    bet_v,
    sea_v,
    wx,
    wy,
    ob_i,
    ob_o,
    ob_a,
    ob_m,
    ob_f,
    own_sem,
    in_sem,
    xs_send,
    xs_recv,
    ys_send,
    ys_recv,
    yx_send,
    yx_recv,
    yb_send,
    yb_recv,
    a_send,
    a_recv,
    r_send,
    r_recv,
    o_send,
    o_recv,
):
    gx, gy = lax.axis_index("gx"), lax.axis_index("gy")
    y, c = gx // 2, gx % 2
    x, z = gy // NZ, gy % NZ
    yp, ym, yo = (y + 1) % YR, (y + YR - 1) % YR, (y + 2) % YR
    sib = (2 * y + 1 - c, gy)

    def col(yy):
        return (2 * yy + c, gy)

    def rcopy(src, dst, ssem, rsem, dev):
        return pltpu.make_async_remote_copy(
            src_ref=src, dst_ref=dst, send_sem=ssem, recv_sem=rsem, device_id=dev, device_id_type=MESH
        )

    def wait(ref, sem):
        pltpu.make_async_copy(ref, ref, sem).wait()

    def worker(kind, u):
        q = (18 * kind + 18 * c + u) % GY
        wx_ = q % NX
        return wx_ * NZ + (q // NX + 2 * wx_) % NZ

    def my_unit(kind):
        q = ((z + 2 * NZ - 2 * x) % NZ) * NX + x
        return (q + 4 * GY - 18 * kind - 18 * c) % GY

    loads = [
        pltpu.make_async_copy(xinv, xbuf, in_sem.at[0]),
        pltpu.make_async_copy(kappa, kap_v, in_sem.at[1]),
        pltpu.make_async_copy(sea, sea_v, in_sem.at[2]),
        pltpu.make_async_copy(sigma, sig_v, in_sem.at[3]),
        pltpu.make_async_copy(beta, bet_v, in_sem.at[4]),
        pltpu.make_async_copy(yinv, Yf.at[pl.ds(gx * YSH, YSH)], in_sem.at[5]),
    ]
    for load in loads[:3]:
        load.start()

    barrier = pltpu.get_barrier_semaphore()
    for i in range(1, GX):
        pl.semaphore_signal(barrier, inc=1, device_id=((gx + i) % GX, gy), device_id_type=MESH)

    @pl.loop(1, GY)
    def _(i):
        pl.semaphore_signal(barrier, inc=1, device_id=(gx, (gy + i) % GY), device_id_type=MESH)

    pl.semaphore_wait(barrier, GX + GY - 2)

    def tile_src(s, k):
        return ctrl.at[k] if s == 0 else F.at[k]

    def x_own_sends(s, k):
        src = tile_src(s, k)
        dst = G.at[s, k, y, c]
        rcopy(src, dst, xs_send.at[s, k, 0], xs_recv.at[s, k, 0], col(yp)).start()
        rcopy(src, dst, xs_send.at[s, k, 1], xs_recv.at[s, k, 1], col(ym)).start()
        rcopy(src, dst, xs_send.at[s, k, 2], xs_recv.at[s, k, 2], sib).start()
        pltpu.make_async_copy(src, dst, own_sem.at[s, k]).start()

    def x_pass(s, k, i):
        piece = G.at[s, k, ym if i == 0 else yp, c]
        wait(piece, xs_recv.at[s, k, i])
        part = piece.at[pl.ds(i * HALF, HALF)]
        rcopy(part, part, xs_send.at[s, k, 3 + i], xs_recv.at[s, k, 3 + i], col(yp if i == 0 else ym)).start()
        rcopy(piece, piece, xs_send.at[s, k, 5 + i], xs_recv.at[s, k, 5 + i], sib).start()

    def x_pass_far(s, k, i):
        part = G.at[s, k, yo, c, pl.ds(i * HALF, HALF)]
        wait(part, xs_recv.at[s, k, 3 + i])
        rcopy(part, part, xs_send.at[s, k, 7 + i], xs_recv.at[s, k, 7 + i], sib).start()

    def x_chunk(s, k, yy, first):
        lhs = jnp.concatenate(
            [G[s, k, yy, 0].reshape(LEV * ROWS, COLS), G[s, k, yy, 1].reshape(LEV * ROWS, COLS)], axis=1
        )
        hi, lo = split2(lhs)
        rhs = XT[pl.ds(pl.multiple_of(yy * 2 * COLS, 2 * COLS), 2 * COLS), :]
        p = jnp.dot(hi, rhs, preferred_element_type=F32)
        q = jnp.dot(lo, rhs[:, :COLS], preferred_element_type=F32)
        val = (p[:, :COLS] + p[:, COLS:]) + q
        if first:
            acc[...] = val
        else:
            acc[...] += val

    def x_finish(s, k):
        for lb in range(LB):
            m = sea_v[:, lb * LANES : (lb + 1) * LANES].astype(F32)
            for f in range(LEV):
                xout[s, k, f * LB + lb] = m * acc[f * ROWS : (f + 1) * ROWS, lb * LANES : (lb + 1) * LANES]

        @pl.loop(0, UNITS)
        def _(u):
            g = worker(k, u)
            src = xout.at[s, k, u]
            dst = U.at[s, k, pl.ds(pl.multiple_of(gy * ROWS, ROWS), ROWS)]

            @pl.when(g != gy)
            def _():
                rcopy(src, dst, a_send.at[s, k], a_recv.at[s, k], (gx, g)).start()

            @pl.when(g == gy)
            def _():
                pltpu.make_async_copy(src, dst, a_recv.at[s, k]).start()

    def y_phase(s, k):
        unit = my_unit(k)

        @pl.when(unit < UNITS)
        def _():
            wait(U.at[s, k], a_recv.at[s, k])
            hi, lo = split2(U[s, k])
            W[:, :LANES] = hi
            W[:, LANES:] = lo

            @pl.loop(0, 4)
            def _(m):
                rows = pl.ds(pl.multiple_of(m * 8 * ROWS, 8 * ROWS), 8 * ROWS)
                p = jnp.dot(Yhi[rows, :], W[...], preferred_element_type=F32)
                q = jnp.dot(Ylo[rows, :], W[:, :LANES], preferred_element_type=F32)
                yout[s, k, rows] = (p[:, :LANES] + p[:, LANES:]) + q

                @pl.loop(0, 8)
                def _(i):
                    g = m * 8 + i
                    src = yout.at[s, k, pl.ds(pl.multiple_of(g * ROWS, ROWS), ROWS)]
                    dst = R.at[s, k, unit]

                    @pl.when(g != gy)
                    def _():
                        rcopy(src, dst, r_send.at[s, k], r_recv.at[s, k], (gx, g)).start()

                    @pl.when(g == gy)
                    def _():
                        pltpu.make_async_copy(src, dst, r_recv.at[s, k]).start()

    def solve(s, k, lb):
        sl = slice(lb * LANES, (lb + 1) * LANES)
        m = sea_v[:, sl].astype(F32)
        d = []
        for l in range(LEV):
            v = R[s, k, l * LB + lb] * m
            if l > 0:
                v = v + kap_v[l - 1, :, sl] * d[-1]
            d.append(v * rp[l, :, sl])
        u = [d[-1]]
        for l in range(LEV - 2, -1, -1):
            u.insert(0, d[l] + cs[l, :, sl] * u[0])
        return u

    def interp_rows(vals, base):
        hi, lo = split2(vals.reshape(-1, COLS))
        p = jnp.dot(hi, wx[...], preferred_element_type=F32)
        q = jnp.dot(lo, wx[:, :SLOTS], preferred_element_type=F32)
        v = ((p[:, :SLOTS] + p[:, SLOTS:]) + q).reshape(-1, ROWS, SLOTS)
        for i in range(v.shape[0]):
            ob_i[pl.ds(base + i, 1), :] = jnp.sum(v[i] * wy[...], axis=0, keepdims=True)

    x_own_sends(0, 0)
    yrow = pl.multiple_of(x * YSB, YSB)

    def yblock(shard, xx, n=1):
        return Yf.at[pl.ds(pl.multiple_of(shard * YSH + xx * YSB, YSB), n * YSB)]

    for i, yy in enumerate((yp, ym, yo)):
        rcopy(yinv.at[pl.ds(yrow, YSB)], yblock(gx, x), ys_send.at[i], ys_recv.at[i], col(yy)).start()
    rcopy(yinv, yblock(gx, 0, NX), yb_send.at[0], yb_recv, sib).start()
    for load in loads[3:]:
        load.start()

    loads[1].wait()
    loads[2].wait()
    for lb in range(LB):
        sl = slice(lb * LANES, (lb + 1) * LANES)
        prev = None
        for l in range(LEV):
            diag = 1.0
            if l > 0:
                diag = diag + kap_v[l - 1, :, sl]
            if l < LEV - 1:
                diag = diag + kap_v[l, :, sl]
            pivot = diag if l == 0 else diag - kap_v[l - 1, :, sl] * prev
            rec = 1.0 / pivot
            rp[l, :, sl] = rec
            if l < LEV - 1:
                prev = kap_v[l, :, sl] * rec
                cs[l, :, sl] = prev

    loads[0].wait()

    @pl.loop(0, NLON // 256)
    def _(j):
        at = pl.ds(pl.multiple_of(j * 256, 256), 256)
        hi, lo = split2(xbuf[:, at].T)
        XT[at, :COLS] = hi
        XT[at, COLS:] = lo

    def x_phase(s, k, after_pass, before_end):
        wait(G.at[s, k, y, c], own_sem.at[s, k])
        wait(G.at[s, k, y, 1 - c], xs_recv.at[s, k, 2])
        x_chunk(s, k, y, True)
        x_pass(s, k, 0)
        x_pass(s, k, 1)
        after_pass()
        wait(G.at[s, k, ym, 1 - c], xs_recv.at[s, k, 5])
        x_chunk(s, k, ym, False)
        wait(G.at[s, k, yp, 1 - c], xs_recv.at[s, k, 6])
        x_chunk(s, k, yp, False)
        before_end()
        x_pass_far(s, k, 0)
        x_pass_far(s, k, 1)
        for i in range(2):
            wait(G.at[s, k, yo, 1 - c, pl.ds(i * HALF, HALF)], xs_recv.at[s, k, 7 + i])
        x_chunk(s, k, yo, False)
        x_finish(s, k)

    def y_first():
        x_own_sends(0, 1)
        for i, yy in enumerate((ym, yp, yo)):
            block = yblock(2 * yy + c, x)
            wait(block, ys_recv.at[i])
            for j in range(1, NX):
                rcopy(block, block, yx_send, yx_recv.at[i], (gx, ((x + j) % NX) * NZ + z)).start()
            rcopy(block, block, yb_send.at[1 + i], yb_recv, sib).start()

    def y_second():
        for i, yy in enumerate((ym, yp, yo)):
            wait(Yf.at[pl.ds(0, 3 * YSB)], yx_recv.at[i])
            for j in range(1, NX):
                block = yblock(2 * yy + c, (x + j) % NX)
                rcopy(block, block, yb_send.at[4 + 3 * i + j - 1], yb_recv, sib).start()

    def nothing():
        pass

    x_phase(0, 0, y_first, nothing)
    x_phase(0, 1, nothing, nothing)
    y_second()

    row = tidx[...]
    three = row >> 7
    trow = (three * 171) >> 9
    tcol = row - trow * COLS
    fx, fy = frac[0:1, :], frac[1:2, :]
    lon = lax.broadcasted_iota(I32, (COLS, SLOTS), 0)
    whi, wlo = split2(jnp.where(lon == tcol, 1.0 - fx, jnp.where(lon == tcol + 1, fx, 0.0)))
    wx[:, :SLOTS] = whi
    wx[:, SLOTS:] = wlo
    lat = lax.broadcasted_iota(I32, (ROWS, SLOTS), 0)
    wy[...] = jnp.where(lat == trow, 1.0 - fy, jnp.where(lat == trow + 1, fy, 0.0))

    loads[5].wait()
    wait(Yf.at[pl.ds(0, 4 * YSH)], yb_recv)

    @pl.loop(0, 8)
    def _(j):
        rows = pl.ds(pl.multiple_of(j * YSH, YSH), YSH)
        hi, lo = split2(Yf[rows, :])
        Yhi[rows, :] = hi
        Ylo[rows, :] = lo

    y_phase(0, 0)
    y_phase(0, 1)

    for k in range(KINDS):
        wait(R.at[0, k], r_recv.at[0, k])
        for lb in range(LB):
            u = solve(0, k, lb)
            for l in range(LEV):
                F[k, l, :, lb * LANES : (lb + 1) * LANES] = u[l]
        x_own_sends(1, k)

    x_phase(1, 0, nothing, nothing)
    x_phase(1, 1, nothing, nothing)
    y_phase(1, 0)
    y_phase(1, 1)

    loads[3].wait()
    loads[4].wait()
    wait(R.at[1, 0], r_recv.at[1, 0])
    for lb in range(LB):
        sl = slice(lb * LANES, (lb + 1) * LANES)
        u = solve(1, 0, lb)
        for l in range(LEV):
            inc[0, l, :, sl] = sig_v[0, l, :, sl] * u[l]
    ob_i[...] = jnp.zeros_like(ob_i)
    interp_rows(inc[0], 0)
    wait(R.at[1, 1], r_recv.at[1, 1])
    for lb in range(LB):
        sl = slice(lb * LANES, (lb + 1) * LANES)
        u = solve(1, 1, lb)
        h = None
        for l in range(LEV):
            t = inc[0, l, :, sl]
            v = sig_v[1, l, :, sl] * u[l] + bet_v[l, :, sl] * t
            inc[1, l, :, sl] = v
            term = ssh[0, l] * t + ssh[1, l] * v
            h = term if h is None else h + term
        height[:, sl] = h
    interp_rows(inc[1], LEV)
    interp_rows(height[...], 2 * LEV)

    own_row = owner[...]
    ia = lax.broadcasted_iota(I32, (SLOTS, SLOTS), 0)
    ib = lax.broadcasted_iota(I32, (SLOTS, SLOTS), 1)
    own_f = own_row.astype(F32)
    own_col = jnp.sum(jnp.where(ia == ib, own_f, 0.0), axis=1, keepdims=True)
    earlier = jnp.where((own_col == own_f) & (ia < ib), 1.0, 0.0)
    rank = jnp.sum(earlier, axis=0, keepdims=True)
    live = lax.broadcasted_iota(I32, (1, SLOTS), 1) < count[0]
    values = jnp.where(live, ob_i[...], 0.0)
    placed = jnp.concatenate(
        [
            jnp.where(rank == 0.0, values, 0.0),
            jnp.where(rank == 1.0, values, 0.0),
            jnp.zeros((LANES - 32, SLOTS), F32),
        ],
        axis=0,
    )
    target = (own_row % GY) * GX + own_row // GY
    pick = jnp.where(ia == target, 1.0, 0.0).astype(BF16)
    hi, mid = split2(placed)
    low = ((placed - hi.astype(F32)) - mid.astype(F32)).astype(BF16)
    dims = (((1,), (1,)), ((), ()))
    ob_o[...] = (
        lax.dot_general(pick, hi, dims, preferred_element_type=F32)
        + lax.dot_general(pick, mid, dims, preferred_element_type=F32)
    ) + lax.dot_general(pick, low, dims, preferred_element_type=F32)

    @pl.loop(0, GY)
    def _(g):
        src = ob_o.at[pl.ds(pl.multiple_of(g * GX, GX), GX)]
        dst = ob_a.at[pl.ds(pl.multiple_of(gy * GX, GX), GX)]

        @pl.when(g != gy)
        def _():
            rcopy(src, dst, o_send.at[0], o_recv.at[0], (gx, g)).start()

        @pl.when(g == gy)
        def _():
            pltpu.make_async_copy(src, dst, o_recv.at[0]).start()

    wait(ob_a, o_recv.at[0])
    for g in range(GX):
        ob_m[g] = ob_a[pl.ds(g, GY, stride=GX), :]
    for g in range(GX):
        src = ob_m.at[g]
        dst = ob_f.at[pl.ds(pl.multiple_of(gx * GY, GY), GY)]

        @pl.when(g != gx)
        def _():
            rcopy(src, dst, o_send.at[1], o_recv.at[1], (g, gy)).start()

        @pl.when(g == gx)
        def _():
            pltpu.make_async_copy(src, dst, o_recv.at[1]).start()

    wait(ob_f, o_recv.at[1])
    turned = ob_f[...].T
    obs[0] = turned[0:REC]
    obs[1] = turned[16 : 16 + REC]

    for s in range(STEPS):
        for k in range(KINDS):
            whole = G.at[s, k, y, c]
            half = G.at[s, k, y, c, pl.ds(0, HALF)]
            for i in range(9):
                wait(half if i in (3, 4, 7, 8) else whole, xs_send.at[s, k, i])
            mine = my_unit(k) < UNITS

            @pl.when(mine)
            def _():
                wait(xout.at[s, k, pl.ds(0, UNITS - 1)], a_send.at[s, k])
                wait(yout.at[s, k, pl.ds(0, (GY - 1) * ROWS)], r_send.at[s, k])

            @pl.when(jnp.logical_not(mine))
            def _():
                wait(xout.at[s, k], a_send.at[s, k])

    for i in range(3):
        wait(yblock(0, 0), ys_send.at[i])
    wait(yblock(0, 0, 9), yx_send)
    wait(yblock(0, 0, NX), yb_send.at[0])
    for i in range(12):
        wait(yblock(0, 0), yb_send.at[1 + i])
    wait(ob_o.at[pl.ds(0, (GY - 1) * GX)], o_send.at[0])
    wait(ob_m.at[pl.ds(0, GX - 1)], o_send.at[1])


def body(
    control, sigma, kappa, beta, sea_mask, x_inverse, y_inverse, ssh_coef, obs_owner, tile_index, obs_frac, obs_count
):
    vmem = pl.BlockSpec(memory_space=pltpu.VMEM)
    smem = pl.BlockSpec(memory_space=pltpu.SMEM)
    hbm = pl.BlockSpec(memory_space=ANY)
    dma = pltpu.SemaphoreType.DMA
    tile = (ROWS, COLS)
    inc, height, obs = pl.pallas_call(
        kernel,
        out_shape=(
            jax.ShapeDtypeStruct((KINDS, LEV) + tile, F32),
            jax.ShapeDtypeStruct(tile, F32),
            jax.ShapeDtypeStruct((CAP, REC, DEV), F32),
        ),
        in_specs=[hbm] * 7 + [smem, vmem, vmem, vmem, smem],
        out_specs=(vmem, vmem, vmem),
        scratch_shapes=[
            pltpu.VMEM((STEPS, KINDS, YR, 2, LEV) + tile, F32),
            pltpu.VMEM((NLON, 2 * COLS), BF16),
            pltpu.VMEM((COLS, NLON), F32),
            pltpu.VMEM((NLAT, NLAT), F32),
            pltpu.VMEM((NLAT, NLAT), BF16),
            pltpu.VMEM((NLAT, NLAT), BF16),
            pltpu.VMEM((STEPS, KINDS, NLAT, LANES), F32),
            pltpu.VMEM((STEPS, KINDS, UNITS, ROWS, LANES), F32),
            pltpu.VMEM((STEPS, KINDS, UNITS, ROWS, LANES), F32),
            pltpu.VMEM((STEPS, KINDS, NLAT, LANES), F32),
            pltpu.VMEM((KINDS, LEV) + tile, F32),
            pltpu.VMEM((LEV * ROWS, COLS), F32),
            pltpu.VMEM((NLAT, 2 * LANES), BF16),
            pltpu.VMEM((LEV - 1,) + tile, F32),
            pltpu.VMEM((LEV,) + tile, F32),
            pltpu.VMEM((KINDS, LEV) + tile, F32),
            pltpu.VMEM((LEV - 1,) + tile, F32),
            pltpu.VMEM((LEV,) + tile, F32),
            pltpu.VMEM(tile, I32),
            pltpu.VMEM((COLS, 2 * SLOTS), BF16),
            pltpu.VMEM((ROWS, SLOTS), F32),
            pltpu.VMEM((16, SLOTS), F32),
            pltpu.VMEM((DEV, LANES), F32),
            pltpu.VMEM((DEV, LANES), F32),
            pltpu.VMEM((GX, GY, LANES), F32),
            pltpu.VMEM((DEV, LANES), F32),
            dma((STEPS, KINDS)),
            dma((6,)),
            dma((STEPS, KINDS, 9)),
            dma((STEPS, KINDS, 9)),
            dma((3,)),
            dma((3,)),
            dma(()),
            dma((3,)),
            dma((13,)),
            dma(()),
            dma((STEPS, KINDS)),
            dma((STEPS, KINDS)),
            dma((STEPS, KINDS)),
            dma((STEPS, KINDS)),
            dma((2,)),
            dma((2,)),
        ],
        compiler_params=pltpu.CompilerParams(
            collective_id=0, has_side_effects=True, vmem_limit_bytes=62 * 1024 * 1024
        ),
        name="covariance",
    )(
        control[0],
        sigma,
        kappa,
        beta,
        sea_mask,
        x_inverse,
        y_inverse,
        ssh_coef,
        obs_owner.reshape(1, SLOTS),
        tile_index.reshape(1, SLOTS),
        obs_frac,
        obs_count,
    )
    return inc[None], height[None], obs


def solution(mesh):
    return jax.shard_map(
        body,
        mesh=mesh,
        in_specs=(
            P(None, None, None, "gy", "gx"),
            P(None, None, "gy", "gx"),
            P(None, "gy", "gx"),
            P(None, "gy", "gx"),
            P("gy", "gx"),
            P("gx", None),
            P("gx", None),
            P(),
            P(("gx", "gy"), None),
            P(("gx", "gy")),
            P(None, ("gx", "gy")),
            P(("gx", "gy")),
        ),
        out_specs=(
            P(None, None, None, "gy", "gx"),
            P(None, "gy", "gx"),
            P(None, None, ("gx", "gy")),
        ),
        check_vma=False,
    )
```

```python
import functools

import jax
import jax.numpy as jnp
from jax import lax
from jax.experimental import pallas as pl
from jax.experimental.pallas import tpu as pltpu
from jax.sharding import PartitionSpec as P

F32, BF16, I32 = jnp.float32, jnp.bfloat16, jnp.int32
MESH = pl.DeviceIdType.MESH
ANY = pl.ANY

STEPS, KINDS, LEV = 2, 2, 6
ROWS, COLS, LANES = 48, 384, 128
LB = COLS // LANES
UNITS = LEV * LB
YR, NX, NZ = 4, 4, 8
GX, GY = 2 * YR, NX * NZ
NLAT, NLON = GY * ROWS, GX * COLS
YSH = NLAT // GX
YSB = YSH // NX
SLOTS, CAP, REC, DEV = 256, 2, 13, GX * GY
PIECES, PLEV = 4, LEV // 2
PUNITS = PLEV * LB


def split2(v):
    hi = v.astype(BF16)
    lo = (v - hi.astype(F32)).astype(BF16)
    return hi, lo


def kernel(
    ctrl,
    sigma,
    kappa,
    beta,
    sea,
    xinv,
    yinv,
    ssh,
    owner,
    tidx,
    frac,
    count,
    inc,
    height,
    obs,
    G,
    XT,
    xbuf,
    Yf,
    Yhi,
    Ylo,
    U,
    R,
    xout,
    yout,
    F,
    acc,
    W,
    cs,
    rp,
    sig_v,
    kap_v,
    bet_v,
    sea_v,
    wx,
    wy,
    ob_i,
    ob_o,
    ob_a,
    ob_m,
    ob_f,
    own_sem,
    in_sem,
    xs_send,
    xs_recv,
    ys_send,
    ys_recv,
    yx_send,
    yx_recv,
    yb_send,
    yb_recv,
    a_send,
    a_recv,
    r_send,
    r_recv,
    o_send,
    o_recv,
):
    gx, gy = lax.axis_index("gx"), lax.axis_index("gy")
    y, c = gx // 2, gx % 2
    x, z = gy // NZ, gy % NZ
    yp, ym, yo = (y + 1) % YR, (y + YR - 1) % YR, (y + 2) % YR
    sib = (2 * y + 1 - c, gy)

    def col(yy):
        return (2 * yy + c, gy)

    def rcopy(src, dst, ssem, rsem, dev):
        return pltpu.make_async_remote_copy(
            src_ref=src, dst_ref=dst, send_sem=ssem, recv_sem=rsem, device_id=dev, device_id_type=MESH
        )

    def wait(ref, sem):
        pltpu.make_async_copy(ref, ref, sem).wait()

    def worker(kind, u):
        q = (18 * kind + 18 * c + u) % GY
        wx_ = q % NX
        return wx_ * NZ + (q // NX + 2 * wx_) % NZ

    def my_unit(kind):
        q = ((z + 2 * NZ - 2 * x) % NZ) * NX + x
        return (q + 4 * GY - 18 * kind - 18 * c) % GY

    loads = [
        pltpu.make_async_copy(xinv, xbuf, in_sem.at[0]),
        pltpu.make_async_copy(kappa, kap_v, in_sem.at[1]),
        pltpu.make_async_copy(sea, sea_v, in_sem.at[2]),
        pltpu.make_async_copy(sigma, sig_v, in_sem.at[3]),
        pltpu.make_async_copy(beta, bet_v, in_sem.at[4]),
        pltpu.make_async_copy(yinv, Yf.at[pl.ds(gx * YSH, YSH)], in_sem.at[5]),
    ]
    for load in loads[:3]:
        load.start()

    barrier = pltpu.get_barrier_semaphore()
    for i in range(1, GX):
        pl.semaphore_signal(barrier, inc=1, device_id=((gx + i) % GX, gy), device_id_type=MESH)

    @pl.loop(1, GY)
    def _(i):
        pl.semaphore_signal(barrier, inc=1, device_id=(gx, (gy + i) % GY), device_id_type=MESH)

    pl.semaphore_wait(barrier, GX + GY - 2)

    def gat(s, p, yy, cc):
        return G.at[s, p, yy, cc]

    def half(ref, i):
        return ref.at[:, pl.ds(i * (ROWS // 2), ROWS // 2)]

    def own(s, p):
        lev = pl.ds((p % 2) * PLEV, PLEV)
        src = ctrl.at[p // 2, lev] if s == 0 else F.at[p // 2, lev]
        dst = gat(s, p, y, c)
        rcopy(src, dst, xs_send.at[s, p, 0], xs_recv.at[s, p, 0], col(yp)).start()
        rcopy(src, dst, xs_send.at[s, p, 1], xs_recv.at[s, p, 1], col(ym)).start()
        rcopy(src, dst, xs_send.at[s, p, 2], xs_recv.at[s, p, 2], sib).start()
        pltpu.make_async_copy(src, dst, own_sem.at[s, p]).start()

    def near(s, p):
        for i, (yy, to) in enumerate(((ym, yp), (yp, ym))):
            piece = gat(s, p, yy, c)
            wait(piece, xs_recv.at[s, p, i])
            part = half(piece, i)
            rcopy(part, part, xs_send.at[s, p, 3 + i], xs_recv.at[s, p, 3 + i], col(to)).start()
            rcopy(piece, piece, xs_send.at[s, p, 5 + i], xs_recv.at[s, p, 5 + i], sib).start()

    def far(s, p):
        for i in range(2):
            part = half(gat(s, p, yo, c), i)
            wait(part, xs_recv.at[s, p, 3 + i])
            rcopy(part, part, xs_send.at[s, p, 7 + i], xs_recv.at[s, p, 7 + i], sib).start()

    def mult(s, p):
        wait(gat(s, p, y, c), own_sem.at[s, p])
        wait(gat(s, p, y, 1 - c), xs_recv.at[s, p, 2])
        wait(gat(s, p, ym, 1 - c), xs_recv.at[s, p, 5])
        wait(gat(s, p, yp, 1 - c), xs_recv.at[s, p, 6])
        acc[...] = jnp.zeros_like(acc)

        @pl.loop(0, YR)
        def _(t):
            yy = (y + t * (t + 1) // 2) % YR

            @pl.when(t == YR - 1)
            def _():
                far(s, p)
                for i in range(2):
                    wait(half(gat(s, p, yo, 1 - c), i), xs_recv.at[s, p, 7 + i])

            lhs = jnp.concatenate([G[s, p, yy, i].reshape(PLEV * ROWS, COLS) for i in range(2)], axis=1)
            hi, lo = split2(lhs)
            rhs = XT[pl.ds(pl.multiple_of(yy * 2 * COLS, 2 * COLS), 2 * COLS), :]
            pr = jnp.dot(hi, rhs, preferred_element_type=F32)
            qr = jnp.dot(lo, rhs[:, :COLS], preferred_element_type=F32)
            acc[...] += (pr[:, :COLS] + pr[:, COLS:]) + qr

        k, first = p // 2, (p % 2) * PUNITS
        for lb in range(LB):
            m = sea_v[:, lb * LANES : (lb + 1) * LANES].astype(F32)
            for f in range(PLEV):
                xout[s, k, first + f * LB + lb] = (
                    m * acc[f * ROWS : (f + 1) * ROWS, lb * LANES : (lb + 1) * LANES]
                )

        @pl.loop(0, PUNITS)
        def _(i):
            u = first + (i + gy) % PUNITS
            g = worker(k, u)
            src = xout.at[s, k, u]
            dst = U.at[s, k, pl.ds(pl.multiple_of(gy * ROWS, ROWS), ROWS)]

            @pl.when(g != gy)
            def _():
                rcopy(src, dst, a_send.at[s, k], a_recv.at[s, k], (gx, g)).start()

            @pl.when(g == gy)
            def _():
                pltpu.make_async_copy(src, dst, a_recv.at[s, k]).start()

    def y_phase(s, k):
        unit = my_unit(k)

        @pl.when(unit < UNITS)
        def _():
            wait(U.at[s, k], a_recv.at[s, k])
            hi, lo = split2(U[s, k])
            W[:, :LANES] = hi
            W[:, LANES:] = lo

            @pl.loop(0, 4)
            def _(step):
                m = (step + gy) % 4
                rows = pl.ds(pl.multiple_of(m * 8 * ROWS, 8 * ROWS), 8 * ROWS)
                p = jnp.dot(Yhi[rows, :], W[...], preferred_element_type=F32)
                q = jnp.dot(Ylo[rows, :], W[:, :LANES], preferred_element_type=F32)
                yout[s, k, rows] = (p[:, :LANES] + p[:, LANES:]) + q

                @pl.loop(0, 8)
                def _(i):
                    g = m * 8 + (i + gy // 4) % 8
                    src = yout.at[s, k, pl.ds(pl.multiple_of(g * ROWS, ROWS), ROWS)]
                    dst = R.at[s, k, unit]

                    @pl.when(g != gy)
                    def _():
                        rcopy(src, dst, r_send.at[s, k], r_recv.at[s, k], (gx, g)).start()

                    @pl.when(g == gy)
                    def _():
                        pltpu.make_async_copy(src, dst, r_recv.at[s, k]).start()

    def solve(s, k, lb):
        sl = slice(lb * LANES, (lb + 1) * LANES)
        m = sea_v[:, sl].astype(F32)
        d = []
        for l in range(LEV):
            v = R[s, k, l * LB + lb] * m
            if l > 0:
                v = v + kap_v[l - 1, :, sl] * d[-1]
            d.append(v * rp[l, :, sl])
        u = [d[-1]]
        for l in range(LEV - 2, -1, -1):
            u.insert(0, d[l] + cs[l, :, sl] * u[0])
        return u

    def interp_rows(vals, base):
        hi, lo = split2(vals.reshape(-1, COLS))
        p = jnp.dot(hi, wx[...], preferred_element_type=F32)
        q = jnp.dot(lo, wx[:, :SLOTS], preferred_element_type=F32)
        v = ((p[:, :SLOTS] + p[:, SLOTS:]) + q).reshape(-1, ROWS, SLOTS)
        for i in range(v.shape[0]):
            ob_i[pl.ds(base + i, 1), :] = jnp.sum(v[i] * wy[...], axis=0, keepdims=True)

    def yblock(shard, xx, n=1):
        return Yf.at[pl.ds(pl.multiple_of(shard * YSH + xx * YSB, YSB), n * YSB)]

    def yhalf(shard, xx, i):
        return Yf.at[pl.ds(pl.multiple_of(shard * YSH + xx * YSB + i * (YSB // 2), YSB // 2), YSB // 2)]

    def row_dev(xx):
        return (gx, xx * NZ + z)

    def to_sib(ref, i):
        rcopy(ref, ref, yb_send.at[i], yb_recv, sib).start()

    def along_x(i, yy):
        block = yblock(2 * yy + c, x)
        rcopy(block, block, yx_send.at[i, 0], yx_recv.at[i, 0], row_dev(xp)).start()
        rcopy(block, block, yx_send.at[i, 1], yx_recv.at[i, 1], row_dev(xm)).start()
        to_sib(block, 1 + i)

    def y_near():
        for i, (yy, to) in enumerate(((ym, yp), (yp, ym))):
            block = yblock(2 * yy + c, x)
            wait(block, ys_recv.at[i])
            part = yhalf(2 * yy + c, x, i)
            rcopy(part, part, ys_send.at[2 + i], ys_recv.at[2 + i], col(to)).start()
            along_x(i, yy)

    def y_far():
        for i in range(2):
            wait(yhalf(2 * yo + c, x, i), ys_recv.at[2 + i])
        along_x(2, yo)

    def x_near(i):
        yy = (ym, yp, yo)[i]
        for j, (xx, to) in enumerate(((xm, xp), (xp, xm))):
            block = yblock(2 * yy + c, xx)
            wait(block, yx_recv.at[i, j])
            part = yhalf(2 * yy + c, xx, j)
            rcopy(part, part, yx_send.at[i, 2 + j], yx_recv.at[i, 2 + j], row_dev(to)).start()
            to_sib(block, 4 + 4 * i + j)

    def x_far(i):
        yy = (ym, yp, yo)[i]
        for j in range(2):
            part = yhalf(2 * yy + c, xo, j)
            wait(part, yx_recv.at[i, 2 + j])
            to_sib(part, 6 + 4 * i + j)

    def y_split(cc):
        @pl.loop(0, YR)
        def _(j):
            rows = pl.ds(pl.multiple_of((2 * j + cc) * YSH, YSH), YSH)
            hi, lo = split2(Yf[rows, :])
            Yhi[rows, :] = hi
            Ylo[rows, :] = lo

    def turn(lo_, hi_):
        @pl.loop(lo_, hi_)
        def _(j):
            at = pl.ds(pl.multiple_of(j * 256, 256), 256)
            hi, lo = split2(xbuf[:, at].T)
            XT[at, :COLS] = hi
            XT[at, COLS:] = lo

    xp, xm, xo = (x + 1) % NX, (x + NX - 1) % NX, (x + 2) % NX
    yrow = yinv.at[pl.ds(pl.multiple_of(x * YSB, YSB), YSB)]
    for i, yy in enumerate((yp, ym)):
        rcopy(yrow, yblock(gx, x), ys_send.at[i], ys_recv.at[i], col(yy)).start()
    own(0, 0)
    rcopy(yinv, yblock(gx, 0, NX), yb_send.at[0], yb_recv, sib).start()
    for load in loads[3:]:
        load.start()

    loads[1].wait()
    loads[2].wait()
    for lb in range(LB):
        sl = slice(lb * LANES, (lb + 1) * LANES)
        prev = None
        for l in range(LEV):
            diag = 1.0
            if l > 0:
                diag = diag + kap_v[l - 1, :, sl]
            if l < LEV - 1:
                diag = diag + kap_v[l, :, sl]
            pivot = diag if l == 0 else diag - kap_v[l - 1, :, sl] * prev
            rec = 1.0 / pivot
            rp[l, :, sl] = rec
            if l < LEV - 1:
                prev = kap_v[l, :, sl] * rec
                cs[l, :, sl] = prev

    loads[0].wait()
    turn(0, 6)
    y_near()
    own(0, 1)
    turn(6, 12)
    near(0, 0)
    own(0, 2)
    y_far()
    mult(0, 0)
    near(0, 1)
    own(0, 3)
    x_near(0)
    mult(0, 1)
    near(0, 2)
    x_near(1)
    x_far(0)
    mult(0, 2)
    near(0, 3)
    x_near(2)
    x_far(1)
    mult(0, 3)
    x_far(2)

    row = tidx[...]
    three = row >> 7
    trow = (three * 171) >> 9
    tcol = row - trow * COLS
    fx, fy = frac[0:1, :], frac[1:2, :]
    lon = lax.broadcasted_iota(I32, (COLS, SLOTS), 0)
    whi, wlo = split2(jnp.where(lon == tcol, 1.0 - fx, jnp.where(lon == tcol + 1, fx, 0.0)))
    wx[:, :SLOTS] = whi
    wx[:, SLOTS:] = wlo
    lat = lax.broadcasted_iota(I32, (ROWS, SLOTS), 0)
    wy[...] = jnp.where(lat == trow, 1.0 - fy, jnp.where(lat == trow + 1, fy, 0.0))

    loads[5].wait()
    y_split(c)
    wait(Yf.at[pl.ds(0, 4 * YSH)], yb_recv)
    y_split(1 - c)
    y_phase(0, 0)
    y_phase(0, 1)

    def first_solve(k):
        wait(R.at[0, k], r_recv.at[0, k])
        for lb in range(LB):
            u = solve(0, k, lb)
            for l in range(LEV):
                F[k, l, :, lb * LANES : (lb + 1) * LANES] = u[l]

    first_solve(0)
    own(1, 0)
    own(1, 1)
    near(1, 0)
    first_solve(1)
    own(1, 2)
    mult(1, 0)
    near(1, 1)
    own(1, 3)
    mult(1, 1)
    near(1, 2)
    mult(1, 2)
    y_phase(1, 0)
    near(1, 3)
    mult(1, 3)

    loads[3].wait()
    loads[4].wait()
    wait(R.at[1, 0], r_recv.at[1, 0])
    for lb in range(LB):
        sl = slice(lb * LANES, (lb + 1) * LANES)
        u = solve(1, 0, lb)
        for l in range(LEV):
            inc[0, l, :, sl] = sig_v[0, l, :, sl] * u[l]
    ob_i[...] = jnp.zeros_like(ob_i)
    interp_rows(inc[0], 0)
    y_phase(1, 1)
    wait(R.at[1, 1], r_recv.at[1, 1])
    for lb in range(LB):
        sl = slice(lb * LANES, (lb + 1) * LANES)
        u = solve(1, 1, lb)
        h = None
        for l in range(LEV):
            t = inc[0, l, :, sl]
            v = sig_v[1, l, :, sl] * u[l] + bet_v[l, :, sl] * t
            inc[1, l, :, sl] = v
            term = ssh[0, l] * t + ssh[1, l] * v
            h = term if h is None else h + term
        height[:, sl] = h
    interp_rows(inc[1], LEV)
    interp_rows(height[...], 2 * LEV)

    own_row = owner[...]
    ia = lax.broadcasted_iota(I32, (SLOTS, SLOTS), 0)
    ib = lax.broadcasted_iota(I32, (SLOTS, SLOTS), 1)
    own_f = own_row.astype(F32)
    own_col = jnp.sum(jnp.where(ia == ib, own_f, 0.0), axis=1, keepdims=True)
    earlier = jnp.where((own_col == own_f) & (ia < ib), 1.0, 0.0)
    rank = jnp.sum(earlier, axis=0, keepdims=True)
    live = lax.broadcasted_iota(I32, (1, SLOTS), 1) < count[0]
    values = jnp.where(live, ob_i[...], 0.0)
    placed = jnp.concatenate(
        [
            jnp.where(rank == 0.0, values, 0.0),
            jnp.where(rank == 1.0, values, 0.0),
            jnp.zeros((LANES - 32, SLOTS), F32),
        ],
        axis=0,
    )
    target = (own_row % GY) * GX + own_row // GY
    pick = jnp.where(ia == target, 1.0, 0.0).astype(BF16)
    hi, mid = split2(placed)
    low = ((placed - hi.astype(F32)) - mid.astype(F32)).astype(BF16)
    dims = (((1,), (1,)), ((), ()))
    ob_o[...] = (
        lax.dot_general(pick, hi, dims, preferred_element_type=F32)
        + lax.dot_general(pick, mid, dims, preferred_element_type=F32)
    ) + lax.dot_general(pick, low, dims, preferred_element_type=F32)

    @pl.loop(0, GY)
    def _(g):
        src = ob_o.at[pl.ds(pl.multiple_of(g * GX, GX), GX)]
        dst = ob_a.at[pl.ds(pl.multiple_of(gy * GX, GX), GX)]

        @pl.when(g != gy)
        def _():
            rcopy(src, dst, o_send.at[0], o_recv.at[0], (gx, g)).start()

        @pl.when(g == gy)
        def _():
            pltpu.make_async_copy(src, dst, o_recv.at[0]).start()

    wait(ob_a, o_recv.at[0])
    for g in range(GX):
        ob_m[g] = ob_a[pl.ds(g, GY, stride=GX), :]
    for g in range(GX):
        src = ob_m.at[g]
        dst = ob_f.at[pl.ds(pl.multiple_of(gx * GY, GY), GY)]

        @pl.when(g != gx)
        def _():
            rcopy(src, dst, o_send.at[1], o_recv.at[1], (g, gy)).start()

        @pl.when(g == gx)
        def _():
            pltpu.make_async_copy(src, dst, o_recv.at[1]).start()

    wait(ob_f, o_recv.at[1])
    turned = ob_f[...].T
    obs[0] = turned[0:REC]
    obs[1] = turned[16 : 16 + REC]

    for s in range(STEPS):
        for p in range(PIECES):
            whole = gat(s, p, y, c)
            for i in range(9):
                wait(half(whole, 0) if i in (3, 4, 7, 8) else whole, xs_send.at[s, p, i])
        for k in range(KINDS):
            mine = my_unit(k) < UNITS

            @pl.when(mine)
            def _():
                wait(xout.at[s, k, pl.ds(0, UNITS - 1)], a_send.at[s, k])
                wait(yout.at[s, k, pl.ds(0, (GY - 1) * ROWS)], r_send.at[s, k])

            @pl.when(jnp.logical_not(mine))
            def _():
                wait(xout.at[s, k], a_send.at[s, k])

    for i in range(4):
        wait(yblock(0, 0) if i < 2 else yhalf(0, 0, 0), ys_send.at[i])
    for i in range(3):
        for j in range(4):
            wait(yblock(0, 0) if j < 2 else yhalf(0, 0, 0), yx_send.at[i, j])
            wait(yblock(0, 0) if j < 2 else yhalf(0, 0, 0), yb_send.at[4 + 4 * i + j])
        wait(yblock(0, 0), yb_send.at[1 + i])
    wait(yblock(0, 0, NX), yb_send.at[0])
    wait(ob_o.at[pl.ds(0, (GY - 1) * GX)], o_send.at[0])
    wait(ob_m.at[pl.ds(0, GX - 1)], o_send.at[1])


def body(
    control, sigma, kappa, beta, sea_mask, x_inverse, y_inverse, ssh_coef, obs_owner, tile_index, obs_frac, obs_count
):
    vmem = pl.BlockSpec(memory_space=pltpu.VMEM)
    smem = pl.BlockSpec(memory_space=pltpu.SMEM)
    hbm = pl.BlockSpec(memory_space=ANY)
    dma = pltpu.SemaphoreType.DMA
    tile = (ROWS, COLS)
    inc, height, obs = pl.pallas_call(
        kernel,
        out_shape=(
            jax.ShapeDtypeStruct((KINDS, LEV) + tile, F32),
            jax.ShapeDtypeStruct(tile, F32),
            jax.ShapeDtypeStruct((CAP, REC, DEV), F32),
        ),
        in_specs=[hbm] * 7 + [smem, vmem, vmem, vmem, smem],
        out_specs=(vmem, vmem, vmem),
        scratch_shapes=[
            pltpu.VMEM((STEPS, PIECES, YR, 2, PLEV) + tile, F32),
            pltpu.VMEM((NLON, 2 * COLS), BF16),
            pltpu.VMEM((COLS, NLON), F32),
            pltpu.VMEM((NLAT, NLAT), F32),
            pltpu.VMEM((NLAT, NLAT), BF16),
            pltpu.VMEM((NLAT, NLAT), BF16),
            pltpu.VMEM((STEPS, KINDS, NLAT, LANES), F32),
            pltpu.VMEM((STEPS, KINDS, UNITS, ROWS, LANES), F32),
            pltpu.VMEM((STEPS, KINDS, UNITS, ROWS, LANES), F32),
            pltpu.VMEM((STEPS, KINDS, NLAT, LANES), F32),
            pltpu.VMEM((KINDS, LEV) + tile, F32),
            pltpu.VMEM((PLEV * ROWS, COLS), F32),
            pltpu.VMEM((NLAT, 2 * LANES), BF16),
            pltpu.VMEM((LEV - 1,) + tile, F32),
            pltpu.VMEM((LEV,) + tile, F32),
            pltpu.VMEM((KINDS, LEV) + tile, F32),
            pltpu.VMEM((LEV - 1,) + tile, F32),
            pltpu.VMEM((LEV,) + tile, F32),
            pltpu.VMEM(tile, I32),
            pltpu.VMEM((COLS, 2 * SLOTS), BF16),
            pltpu.VMEM((ROWS, SLOTS), F32),
            pltpu.VMEM((16, SLOTS), F32),
            pltpu.VMEM((DEV, LANES), F32),
            pltpu.VMEM((DEV, LANES), F32),
            pltpu.VMEM((GX, GY, LANES), F32),
            pltpu.VMEM((DEV, LANES), F32),
            dma((STEPS, PIECES)),
            dma((6,)),
            dma((STEPS, PIECES, 9)),
            dma((STEPS, PIECES, 9)),
            dma((4,)),
            dma((4,)),
            dma((3, 4)),
            dma((3, 4)),
            dma((16,)),
            dma(()),
            dma((STEPS, KINDS)),
            dma((STEPS, KINDS)),
            dma((STEPS, KINDS)),
            dma((STEPS, KINDS)),
            dma((2,)),
            dma((2,)),
        ],
        compiler_params=pltpu.CompilerParams(
            collective_id=0, has_side_effects=True, vmem_limit_bytes=62 * 1024 * 1024
        ),
        name="covariance",
    )(
        control[0],
        sigma,
        kappa,
        beta,
        sea_mask,
        x_inverse,
        y_inverse,
        ssh_coef,
        obs_owner.reshape(1, SLOTS),
        tile_index.reshape(1, SLOTS),
        obs_frac,
        obs_count,
    )
    return inc[None], height[None], obs


def solution(mesh):
    return jax.shard_map(
        body,
        mesh=mesh,
        in_specs=(
            P(None, None, None, "gy", "gx"),
            P(None, None, "gy", "gx"),
            P(None, "gy", "gx"),
            P(None, "gy", "gx"),
            P("gy", "gx"),
            P("gx", None),
            P("gx", None),
            P(),
            P(("gx", "gy"), None),
            P(("gx", "gy")),
            P(None, ("gx", "gy")),
            P(("gx", "gy")),
        ),
        out_specs=(
            P(None, None, None, "gy", "gx"),
            P(None, "gy", "gx"),
            P(None, None, ("gx", "gy")),
        ),
        check_vma=False,
    )
```

```python
import functools

import jax
import jax.numpy as jnp
from jax import lax
from jax.experimental import pallas as pl
from jax.experimental.pallas import tpu as pltpu
from jax.sharding import PartitionSpec as P

F32, BF16, I32 = jnp.float32, jnp.bfloat16, jnp.int32
MESH = pl.DeviceIdType.MESH
ANY = pl.ANY

STEPS, KINDS, LEV = 2, 2, 6
ROWS, COLS, LANES = 48, 384, 128
LB = COLS // LANES
UNITS = LEV * LB
YR, NX, NZ = 4, 4, 8
GX, GY = 2 * YR, NX * NZ
NLAT, NLON = GY * ROWS, GX * COLS
YSH = NLAT // GX
YSB = YSH // NX
SLOTS, CAP, REC, DEV = 256, 2, 13, GX * GY
PIECES, PLEV = 4, LEV // 2
PUNITS = PLEV * LB


def split2(v):
    hi = v.astype(BF16)
    lo = (v - hi.astype(F32)).astype(BF16)
    return hi, lo


def kernel(
    ctrl,
    sigma,
    kappa,
    beta,
    sea,
    xinv,
    yinv,
    ssh,
    owner,
    tidx,
    frac,
    count,
    inc,
    height,
    obs,
    G,
    XT,
    xbuf,
    Yf,
    Yhi,
    Ylo,
    U,
    R,
    xout,
    yout,
    F,
    acc,
    W,
    cs,
    rp,
    sig_v,
    kap_v,
    bet_v,
    sea_v,
    wx,
    wy,
    ob_i,
    ob_o,
    ob_a,
    ob_m,
    ob_f,
    own_sem,
    in_sem,
    xs_send,
    xs_recv,
    ys_send,
    ys_recv,
    yx_send,
    yx_recv,
    yb_send,
    yb_recv,
    a_send,
    a_recv,
    r_send,
    r_recv,
    o_send,
    o_recv,
):
    gx, gy = lax.axis_index("gx"), lax.axis_index("gy")
    y, c = gx // 2, gx % 2
    x, z = gy // NZ, gy % NZ
    yp, ym, yo = (y + 1) % YR, (y + YR - 1) % YR, (y + 2) % YR
    sib = (2 * y + 1 - c, gy)

    def col(yy):
        return (2 * yy + c, gy)

    def rcopy(src, dst, ssem, rsem, dev):
        return pltpu.make_async_remote_copy(
            src_ref=src, dst_ref=dst, send_sem=ssem, recv_sem=rsem, device_id=dev, device_id_type=MESH
        )

    def wait(ref, sem):
        pltpu.make_async_copy(ref, ref, sem).wait()

    def worker(kind, u):
        q = (18 * kind + 18 * c + u) % GY
        wx_ = q % NX
        return wx_ * NZ + (q // NX + 2 * wx_) % NZ

    def my_unit(kind):
        q = ((z + 2 * NZ - 2 * x) % NZ) * NX + x
        return (q + 4 * GY - 18 * kind - 18 * c) % GY

    loads = [
        pltpu.make_async_copy(xinv, xbuf, in_sem.at[0]),
        pltpu.make_async_copy(kappa, kap_v, in_sem.at[1]),
        pltpu.make_async_copy(sea, sea_v, in_sem.at[2]),
        pltpu.make_async_copy(sigma, sig_v, in_sem.at[3]),
        pltpu.make_async_copy(beta, bet_v, in_sem.at[4]),
        pltpu.make_async_copy(yinv, Yf.at[pl.ds(gx * YSH, YSH)], in_sem.at[5]),
    ]
    for load in loads[:3]:
        load.start()

    barrier = pltpu.get_barrier_semaphore()
    for i in range(1, GX):
        pl.semaphore_signal(barrier, inc=1, device_id=((gx + i) % GX, gy), device_id_type=MESH)

    @pl.loop(1, GY)
    def _(i):
        pl.semaphore_signal(barrier, inc=1, device_id=(gx, (gy + i) % GY), device_id_type=MESH)

    pl.semaphore_wait(barrier, GX + GY - 2)

    def gat(s, p, yy, cc):
        return G.at[s, p, yy, cc]

    def half(ref, i):
        return ref.at[:, pl.ds(i * (ROWS // 2), ROWS // 2)]

    def own(s, p):
        lev = pl.ds((p % 2) * PLEV, PLEV)
        src = ctrl.at[p // 2, lev] if s == 0 else F.at[p // 2, lev]
        dst = gat(s, p, y, c)
        rcopy(src, dst, xs_send.at[s, p, 0], xs_recv.at[s, p, 0], col(yp)).start()
        rcopy(src, dst, xs_send.at[s, p, 1], xs_recv.at[s, p, 1], col(ym)).start()
        rcopy(src, dst, xs_send.at[s, p, 2], xs_recv.at[s, p, 2], sib).start()
        pltpu.make_async_copy(src, dst, own_sem.at[s, p]).start()

    def near(s, p):
        for i, (yy, to) in enumerate(((ym, yp), (yp, ym))):
            piece = gat(s, p, yy, c)
            wait(piece, xs_recv.at[s, p, i])
            part = half(piece, i)
            rcopy(part, part, xs_send.at[s, p, 3 + i], xs_recv.at[s, p, 3 + i], col(to)).start()
            rcopy(piece, piece, xs_send.at[s, p, 5 + i], xs_recv.at[s, p, 5 + i], sib).start()

    def far(s, p):
        for i in range(2):
            part = half(gat(s, p, yo, c), i)
            wait(part, xs_recv.at[s, p, 3 + i])
            rcopy(part, part, xs_send.at[s, p, 7 + i], xs_recv.at[s, p, 7 + i], sib).start()

    def mult(s, p):
        wait(gat(s, p, y, c), own_sem.at[s, p])
        wait(gat(s, p, y, 1 - c), xs_recv.at[s, p, 2])
        wait(gat(s, p, ym, 1 - c), xs_recv.at[s, p, 5])
        wait(gat(s, p, yp, 1 - c), xs_recv.at[s, p, 6])
        acc[...] = jnp.zeros_like(acc)

        @pl.loop(0, YR)
        def _(t):
            yy = (y + t * (t + 1) // 2) % YR

            @pl.when(t == YR - 1)
            def _():
                for i in range(2):
                    wait(half(gat(s, p, yo, 1 - c), i), xs_recv.at[s, p, 7 + i])

            lhs = jnp.concatenate([G[s, p, yy, i].reshape(PLEV * ROWS, COLS) for i in range(2)], axis=1)
            hi, lo = split2(lhs)
            rhs = XT[pl.ds(pl.multiple_of(yy * 2 * COLS, 2 * COLS), 2 * COLS), :]
            pr = jnp.dot(hi, rhs, preferred_element_type=F32)
            qr = jnp.dot(lo, rhs[:, :COLS], preferred_element_type=F32)
            acc[...] += (pr[:, :COLS] + pr[:, COLS:]) + qr

        k, first = p // 2, (p % 2) * PUNITS
        for lb in range(LB):
            m = sea_v[:, lb * LANES : (lb + 1) * LANES].astype(F32)
            for f in range(PLEV):
                xout[s, k, first + f * LB + lb] = (
                    m * acc[f * ROWS : (f + 1) * ROWS, lb * LANES : (lb + 1) * LANES]
                )

        @pl.loop(0, PUNITS)
        def _(i):
            u = first + (i + gy) % PUNITS
            g = worker(k, u)
            src = xout.at[s, k, u]
            dst = U.at[s, k, pl.ds(pl.multiple_of(gy * ROWS, ROWS), ROWS)]

            @pl.when(g != gy)
            def _():
                rcopy(src, dst, a_send.at[s, k], a_recv.at[s, k], (gx, g)).start()

            @pl.when(g == gy)
            def _():
                pltpu.make_async_copy(src, dst, a_recv.at[s, k]).start()

    def y_load(s, k):
        @pl.when(my_unit(k) < UNITS)
        def _():
            wait(U.at[s, k], a_recv.at[s, k])
            hi, lo = split2(U[s, k])
            W[:, :LANES] = hi
            W[:, LANES:] = lo

    def y_rows(s, k, begin, end):
        unit = my_unit(k)

        @pl.when(unit < UNITS)
        def _():
            @pl.loop(begin, end)
            def _(t):
                m = (y + t * (7 - t) // 2) % YR
                rows = pl.ds(pl.multiple_of(m * 8 * ROWS, 8 * ROWS), 8 * ROWS)
                p = jnp.dot(Yhi[rows, :], W[...], preferred_element_type=F32)
                q = jnp.dot(Ylo[rows, :], W[:, :LANES], preferred_element_type=F32)
                yout[s, k, rows] = (p[:, :LANES] + p[:, LANES:]) + q

                @pl.loop(0, 8)
                def _(i):
                    g = m * 8 + (i + gy) % 8
                    src = yout.at[s, k, pl.ds(pl.multiple_of(g * ROWS, ROWS), ROWS)]
                    dst = R.at[s, k, unit]

                    @pl.when(g != gy)
                    def _():
                        rcopy(src, dst, r_send.at[s, k], r_recv.at[s, k], (gx, g)).start()

                    @pl.when(g == gy)
                    def _():
                        pltpu.make_async_copy(src, dst, r_recv.at[s, k]).start()

    def y_phase(s, k):
        y_load(s, k)
        y_rows(s, k, 0, YR)

    def solve(s, k, lb):
        sl = slice(lb * LANES, (lb + 1) * LANES)
        m = sea_v[:, sl].astype(F32)
        d = []
        for l in range(LEV):
            v = R[s, k, l * LB + lb] * m
            if l > 0:
                v = v + kap_v[l - 1, :, sl] * d[-1]
            d.append(v * rp[l, :, sl])
        u = [d[-1]]
        for l in range(LEV - 2, -1, -1):
            u.insert(0, d[l] + cs[l, :, sl] * u[0])
        return u

    def interp_rows(vals, base):
        hi, lo = split2(vals.reshape(-1, COLS))
        p = jnp.dot(hi, wx[...], preferred_element_type=F32)
        q = jnp.dot(lo, wx[:, :SLOTS], preferred_element_type=F32)
        v = ((p[:, :SLOTS] + p[:, SLOTS:]) + q).reshape(-1, ROWS, SLOTS)
        for i in range(v.shape[0]):
            ob_i[pl.ds(base + i, 1), :] = jnp.sum(v[i] * wy[...], axis=0, keepdims=True)

    def yblock(shard, xx, n=1):
        return Yf.at[pl.ds(pl.multiple_of(shard * YSH + xx * YSB, YSB), n * YSB)]

    def yhalf(shard, xx, i):
        return Yf.at[pl.ds(pl.multiple_of(shard * YSH + xx * YSB + i * (YSB // 2), YSB // 2), YSB // 2)]

    def row_dev(xx):
        return (gx, xx * NZ + z)

    def to_sib(ref, i, group):
        rcopy(ref, ref, yb_send.at[i], yb_recv.at[group], sib).start()

    def along_x(i, yy):
        block = yblock(2 * yy + c, x)
        rcopy(block, block, yx_send.at[i, 0], yx_recv.at[i, 0], row_dev(xp)).start()
        rcopy(block, block, yx_send.at[i, 1], yx_recv.at[i, 1], row_dev(xm)).start()
        to_sib(block, 1 + i, 1 + i)

    def y_near():
        for i, (yy, to) in enumerate(((ym, yp), (yp, ym))):
            block = yblock(2 * yy + c, x)
            wait(block, ys_recv.at[i])
            part = yhalf(2 * yy + c, x, i)
            rcopy(part, part, ys_send.at[2 + i], ys_recv.at[2 + i], col(to)).start()
            along_x(i, yy)

    def y_far():
        for i in range(2):
            wait(yhalf(2 * yo + c, x, i), ys_recv.at[2 + i])
        along_x(2, yo)

    def x_near(i):
        yy = (ym, yp, yo)[i]
        for j, (xx, to) in enumerate(((xm, xp), (xp, xm))):
            block = yblock(2 * yy + c, xx)
            wait(block, yx_recv.at[i, j])
            part = yhalf(2 * yy + c, xx, j)
            rcopy(part, part, yx_send.at[i, 2 + j], yx_recv.at[i, 2 + j], row_dev(to)).start()
            to_sib(block, 4 + 4 * i + j, 1 + i)

    def x_far(i):
        yy = (ym, yp, yo)[i]
        for j in range(2):
            part = yhalf(2 * yy + c, xo, j)
            wait(part, yx_recv.at[i, 2 + j])
            to_sib(part, 6 + 4 * i + j, 1 + i)

    def y_split(group):
        yy = (y, ym, yp, yo)[group]
        wait(yblock(0, 0, NX), yb_recv.at[group])

        @pl.loop(0, 2)
        def _(cc):
            rows = pl.ds(pl.multiple_of((2 * yy + cc) * YSH, YSH), YSH)
            hi, lo = split2(Yf[rows, :])
            Yhi[rows, :] = hi
            Ylo[rows, :] = lo

    def turn(lo_, hi_):
        @pl.loop(lo_, hi_)
        def _(j):
            at = pl.ds(pl.multiple_of(j * 256, 256), 256)
            hi, lo = split2(xbuf[:, at].T)
            XT[at, :COLS] = hi
            XT[at, COLS:] = lo

    xp, xm, xo = (x + 1) % NX, (x + NX - 1) % NX, (x + 2) % NX
    yrow = yinv.at[pl.ds(pl.multiple_of(x * YSB, YSB), YSB)]
    for i, yy in enumerate((yp, ym)):
        rcopy(yrow, yblock(gx, x), ys_send.at[i], ys_recv.at[i], col(yy)).start()
    own(0, 0)
    rcopy(yinv, yblock(gx, 0, NX), yb_send.at[0], yb_recv.at[0], sib).start()
    for load in loads[3:]:
        load.start()

    loads[1].wait()
    loads[2].wait()
    for lb in range(LB):
        sl = slice(lb * LANES, (lb + 1) * LANES)
        prev = None
        for l in range(LEV):
            diag = 1.0
            if l > 0:
                diag = diag + kap_v[l - 1, :, sl]
            if l < LEV - 1:
                diag = diag + kap_v[l, :, sl]
            pivot = diag if l == 0 else diag - kap_v[l - 1, :, sl] * prev
            rec = 1.0 / pivot
            rp[l, :, sl] = rec
            if l < LEV - 1:
                prev = kap_v[l, :, sl] * rec
                cs[l, :, sl] = prev

    def first_solve(k):
        wait(R.at[0, k], r_recv.at[0, k])
        for lb in range(LB):
            u = solve(0, k, lb)
            for l in range(LEV):
                F[k, l, :, lb * LANES : (lb + 1) * LANES] = u[l]

    loads[0].wait()
    turn(0, 6)
    y_near()
    own(0, 1)
    turn(6, 12)
    near(0, 0)
    own(0, 2)
    y_far()
    near(0, 1)
    own(0, 3)
    x_near(0)
    x_near(1)
    far(0, 0)
    mult(0, 0)
    near(0, 2)
    x_near(2)
    far(0, 1)
    mult(0, 1)
    near(0, 3)
    x_far(0)
    far(0, 2)
    mult(0, 2)
    x_far(1)
    far(0, 3)
    loads[5].wait()
    y_split(0)
    y_split(1)
    y_split(2)
    y_load(0, 0)
    y_rows(0, 0, 0, 3)
    mult(0, 3)
    x_far(2)
    y_split(3)
    y_rows(0, 0, 3, 4)
    y_phase(0, 1)

    row = tidx[...]
    three = row >> 7
    trow = (three * 171) >> 9
    tcol = row - trow * COLS
    fx, fy = frac[0:1, :], frac[1:2, :]
    lon = lax.broadcasted_iota(I32, (COLS, SLOTS), 0)
    whi, wlo = split2(jnp.where(lon == tcol, 1.0 - fx, jnp.where(lon == tcol + 1, fx, 0.0)))
    wx[:, :SLOTS] = whi
    wx[:, SLOTS:] = wlo
    lat = lax.broadcasted_iota(I32, (ROWS, SLOTS), 0)
    wy[...] = jnp.where(lat == trow, 1.0 - fy, jnp.where(lat == trow + 1, fy, 0.0))


    first_solve(0)
    own(1, 0)
    own(1, 1)
    near(1, 0)
    near(1, 1)
    far(1, 0)
    first_solve(1)
    own(1, 2)
    own(1, 3)
    mult(1, 0)
    far(1, 1)
    mult(1, 1)
    near(1, 2)
    near(1, 3)
    far(1, 2)
    mult(1, 2)
    far(1, 3)
    mult(1, 3)
    y_phase(1, 0)
    y_phase(1, 1)

    loads[3].wait()
    loads[4].wait()
    wait(R.at[1, 0], r_recv.at[1, 0])
    for lb in range(LB):
        sl = slice(lb * LANES, (lb + 1) * LANES)
        u = solve(1, 0, lb)
        for l in range(LEV):
            inc[0, l, :, sl] = sig_v[0, l, :, sl] * u[l]
    ob_i[...] = jnp.zeros_like(ob_i)
    interp_rows(inc[0], 0)
    wait(R.at[1, 1], r_recv.at[1, 1])
    for lb in range(LB):
        sl = slice(lb * LANES, (lb + 1) * LANES)
        u = solve(1, 1, lb)
        h = None
        for l in range(LEV):
            t = inc[0, l, :, sl]
            v = sig_v[1, l, :, sl] * u[l] + bet_v[l, :, sl] * t
            inc[1, l, :, sl] = v
            term = ssh[0, l] * t + ssh[1, l] * v
            h = term if h is None else h + term
        height[:, sl] = h
    interp_rows(inc[1], LEV)
    interp_rows(height[...], 2 * LEV)

    own_row = owner[...]
    ia = lax.broadcasted_iota(I32, (SLOTS, SLOTS), 0)
    ib = lax.broadcasted_iota(I32, (SLOTS, SLOTS), 1)
    own_f = own_row.astype(F32)
    own_col = jnp.sum(jnp.where(ia == ib, own_f, 0.0), axis=1, keepdims=True)
    earlier = jnp.where((own_col == own_f) & (ia < ib), 1.0, 0.0)
    rank = jnp.sum(earlier, axis=0, keepdims=True)
    live = lax.broadcasted_iota(I32, (1, SLOTS), 1) < count[0]
    values = jnp.where(live, ob_i[...], 0.0)
    ogx, ogy = own_row // GY, own_row % GY
    both = jnp.concatenate([jnp.where(rank == 0.0, values, 0.0), jnp.where(rank == 1.0, values, 0.0)], axis=0)
    placed = jnp.concatenate([jnp.where(ogx % 4 == q, both, 0.0) for q in range(4)], axis=0)
    hi, mid = split2(placed)
    low = ((placed - hi.astype(F32)) - mid.astype(F32)).astype(BF16)
    dims = (((1,), (1,)), ((), ()))
    line = lax.broadcasted_iota(I32, (GY, SLOTS), 0)
    for h in range(2):
        pick = jnp.where((line == ogy) & (ogx // 4 == h), 1.0, 0.0).astype(BF16)
        ob_o[:, h, :] = (
            lax.dot_general(pick, hi, dims, preferred_element_type=F32)
            + lax.dot_general(pick, mid, dims, preferred_element_type=F32)
        ) + lax.dot_general(pick, low, dims, preferred_element_type=F32)

    @pl.loop(0, GY)
    def _(i):
        g = (gy + i) % GY
        src = ob_o.at[g]
        dst = ob_a.at[gy]

        @pl.when(i != 0)
        def _():
            rcopy(src, dst, o_send.at[0], o_recv.at[0], (gx, g)).start()

        @pl.when(i == 0)
        def _():
            pltpu.make_async_copy(src, dst, o_recv.at[0]).start()

    wait(ob_a, o_recv.at[0])
    for g in range(GX):
        part = ob_a[:, g // 4, :]
        ob_m[g] = pltpu.roll(part, (LANES - 32 * (g % 4)) % LANES, 1) if g % 4 else part
    for g in range(GX):
        src = ob_m.at[g]
        dst = ob_f.at[pl.ds(pl.multiple_of(gx * GY, GY), GY)]

        @pl.when(g != gx)
        def _():
            rcopy(src, dst, o_send.at[1], o_recv.at[1], (g, gy)).start()

        @pl.when(g == gx)
        def _():
            pltpu.make_async_copy(src, dst, o_recv.at[1]).start()

    wait(ob_f, o_recv.at[1])
    turned = ob_f[...].T
    obs[:, 0, :] = turned[0:REC]
    obs[:, 1, :] = turned[16 : 16 + REC]

    for s in range(STEPS):
        for p in range(PIECES):
            whole = gat(s, p, y, c)
            for i in range(9):
                wait(half(whole, 0) if i in (3, 4, 7, 8) else whole, xs_send.at[s, p, i])
        for k in range(KINDS):
            mine = my_unit(k) < UNITS

            @pl.when(mine)
            def _():
                wait(xout.at[s, k, pl.ds(0, UNITS - 1)], a_send.at[s, k])
                wait(yout.at[s, k, pl.ds(0, (GY - 1) * ROWS)], r_send.at[s, k])

            @pl.when(jnp.logical_not(mine))
            def _():
                wait(xout.at[s, k], a_send.at[s, k])

    for i in range(4):
        wait(yblock(0, 0) if i < 2 else yhalf(0, 0, 0), ys_send.at[i])
    for i in range(3):
        for j in range(4):
            wait(yblock(0, 0) if j < 2 else yhalf(0, 0, 0), yx_send.at[i, j])
            wait(yblock(0, 0) if j < 2 else yhalf(0, 0, 0), yb_send.at[4 + 4 * i + j])
        wait(yblock(0, 0), yb_send.at[1 + i])
    wait(yblock(0, 0, NX), yb_send.at[0])
    wait(ob_o.at[pl.ds(0, GY - 1)], o_send.at[0])
    wait(ob_m.at[pl.ds(0, GX - 1)], o_send.at[1])


def copy_out(a, b, d, oa, ob, od):
    oa[...] = a[...]
    ob[...] = b[...]
    od[...] = d[...]


def body(
    control, sigma, kappa, beta, sea_mask, x_inverse, y_inverse, ssh_coef, obs_owner, tile_index, obs_frac, obs_count
):
    vmem = pl.BlockSpec(memory_space=pltpu.VMEM)
    smem = pl.BlockSpec(memory_space=pltpu.SMEM)
    hbm = pl.BlockSpec(memory_space=ANY)
    dma = pltpu.SemaphoreType.DMA
    tile = (ROWS, COLS)
    inc, height, obs = pl.pallas_call(
        kernel,
        out_shape=(
            jax.ShapeDtypeStruct((KINDS, LEV) + tile, F32),
            jax.ShapeDtypeStruct(tile, F32),
            jax.ShapeDtypeStruct((REC, CAP, DEV), F32),
        ),
        in_specs=[hbm] * 7 + [smem, vmem, vmem, vmem, smem],
        out_specs=(vmem, vmem, vmem),
        scratch_shapes=[
            pltpu.VMEM((STEPS, PIECES, YR, 2, PLEV) + tile, F32),
            pltpu.VMEM((NLON, 2 * COLS), BF16),
            pltpu.VMEM((COLS, NLON), F32),
            pltpu.VMEM((NLAT, NLAT), F32),
            pltpu.VMEM((NLAT, NLAT), BF16),
            pltpu.VMEM((NLAT, NLAT), BF16),
            pltpu.VMEM((STEPS, KINDS, NLAT, LANES), F32),
            pltpu.VMEM((STEPS, KINDS, UNITS, ROWS, LANES), F32),
            pltpu.VMEM((STEPS, KINDS, UNITS, ROWS, LANES), F32),
            pltpu.VMEM((STEPS, KINDS, NLAT, LANES), F32),
            pltpu.VMEM((KINDS, LEV) + tile, F32),
            pltpu.VMEM((PLEV * ROWS, COLS), F32),
            pltpu.VMEM((NLAT, 2 * LANES), BF16),
            pltpu.VMEM((LEV - 1,) + tile, F32),
            pltpu.VMEM((LEV,) + tile, F32),
            pltpu.VMEM((KINDS, LEV) + tile, F32),
            pltpu.VMEM((LEV - 1,) + tile, F32),
            pltpu.VMEM((LEV,) + tile, F32),
            pltpu.VMEM(tile, I32),
            pltpu.VMEM((COLS, 2 * SLOTS), BF16),
            pltpu.VMEM((ROWS, SLOTS), F32),
            pltpu.VMEM((16, SLOTS), F32),
            pltpu.VMEM((GY, 2, LANES), F32),
            pltpu.VMEM((GY, 2, LANES), F32),
            pltpu.VMEM((GX, GY, LANES), F32),
            pltpu.VMEM((DEV, LANES), F32),
            dma((STEPS, PIECES)),
            dma((6,)),
            dma((STEPS, PIECES, 9)),
            dma((STEPS, PIECES, 9)),
            dma((4,)),
            dma((4,)),
            dma((3, 4)),
            dma((3, 4)),
            dma((16,)),
            dma((4,)),
            dma((STEPS, KINDS)),
            dma((STEPS, KINDS)),
            dma((STEPS, KINDS)),
            dma((STEPS, KINDS)),
            dma((2,)),
            dma((2,)),
        ],
        compiler_params=pltpu.CompilerParams(
            collective_id=0, has_side_effects=True, vmem_limit_bytes=62 * 1024 * 1024
        ),
        name="covariance",
    )(
        control[0],
        sigma,
        kappa,
        beta,
        sea_mask,
        x_inverse,
        y_inverse,
        ssh_coef,
        obs_owner.reshape(1, SLOTS),
        tile_index.reshape(1, SLOTS),
        obs_frac,
        obs_count,
    )
    results = (inc, height, obs)
    inc, height, obs = pl.pallas_call(
        copy_out,
        out_shape=tuple(jax.ShapeDtypeStruct(r.shape, F32) for r in results),
        in_specs=[vmem] * 3,
        out_specs=(vmem,) * 3,
        name="outputs",
    )(*results)
    return inc[None], height[None], jnp.swapaxes(obs, 0, 1)


def solution(mesh):
    return jax.shard_map(
        body,
        mesh=mesh,
        in_specs=(
            P(None, None, None, "gy", "gx"),
            P(None, None, "gy", "gx"),
            P(None, "gy", "gx"),
            P(None, "gy", "gx"),
            P("gy", "gx"),
            P("gx", None),
            P("gx", None),
            P(),
            P(("gx", "gy"), None),
            P(("gx", "gy")),
            P(None, ("gx", "gy")),
            P(("gx", "gy")),
        ),
        out_specs=(
            P(None, None, None, "gy", "gx"),
            P(None, "gy", "gx"),
            P(None, None, ("gx", "gy")),
        ),
        check_vma=False,
    )
```

```python
import functools

import jax
import jax.numpy as jnp
from jax import lax
from jax.experimental import pallas as pl
from jax.experimental.pallas import tpu as pltpu
from jax.sharding import PartitionSpec as P

F32, BF16, I32 = jnp.float32, jnp.bfloat16, jnp.int32
MESH = pl.DeviceIdType.MESH
ANY = pl.ANY

STEPS, KINDS, LEV = 2, 2, 6
ROWS, COLS, LANES = 48, 384, 128
LB = COLS // LANES
UNITS = LEV * LB
YR, NX, NZ = 4, 4, 8
GX, GY = 2 * YR, NX * NZ
NLAT, NLON = GY * ROWS, GX * COLS
YSH = NLAT // GX
YSB = YSH // NX
SLOTS, CAP, REC, DEV = 256, 2, 13, GX * GY
PIECES, PLEV = 4, LEV // 2
PUNITS = PLEV * LB


def split2(v):
    hi = v.astype(BF16)
    lo = (v - hi.astype(F32)).astype(BF16)
    return hi, lo


def kernel(
    ctrl,
    sigma,
    kappa,
    beta,
    sea,
    xinv,
    yinv,
    ssh,
    owner,
    tidx,
    frac,
    count,
    inc,
    height,
    obs,
    G,
    XT,
    xbuf,
    Yf,
    Yhi,
    Ylo,
    U,
    R,
    xout,
    yout,
    F,
    acc,
    W,
    cs,
    rp,
    sig_v,
    kap_v,
    bet_v,
    sea_v,
    wx,
    wy,
    slot,
    picks,
    ob_i,
    ob_o,
    ob_a,
    ob_m,
    ob_f,
    own_sem,
    in_sem,
    xs_send,
    xs_recv,
    ys_send,
    ys_recv,
    yx_send,
    yx_recv,
    yb_send,
    yb_recv,
    a_send,
    a_recv,
    r_send,
    r_recv,
    o_send,
    o_recv,
):
    gx, gy = lax.axis_index("gx"), lax.axis_index("gy")
    y, c = gx // 2, gx % 2
    x, z = gy // NZ, gy % NZ
    yp, ym, yo = (y + 1) % YR, (y + YR - 1) % YR, (y + 2) % YR
    sib = (2 * y + 1 - c, gy)

    def col(yy):
        return (2 * yy + c, gy)

    def rcopy(src, dst, ssem, rsem, dev):
        return pltpu.make_async_remote_copy(
            src_ref=src, dst_ref=dst, send_sem=ssem, recv_sem=rsem, device_id=dev, device_id_type=MESH
        )

    def wait(ref, sem):
        pltpu.make_async_copy(ref, ref, sem).wait()

    def worker(kind, u):
        q = (18 * kind + 18 * c + u) % GY
        wx_ = q % NX
        return wx_ * NZ + (q // NX + 2 * wx_) % NZ

    def my_unit(kind):
        q = ((z + 2 * NZ - 2 * x) % NZ) * NX + x
        return (q + 4 * GY - 18 * kind - 18 * c) % GY

    loads = [
        pltpu.make_async_copy(xinv, xbuf, in_sem.at[0]),
        pltpu.make_async_copy(kappa, kap_v, in_sem.at[1]),
        pltpu.make_async_copy(sea, sea_v, in_sem.at[2]),
        pltpu.make_async_copy(sigma, sig_v, in_sem.at[3]),
        pltpu.make_async_copy(beta, bet_v, in_sem.at[4]),
        pltpu.make_async_copy(yinv, Yf.at[pl.ds(gx * YSH, YSH)], in_sem.at[5]),
    ]
    for load in loads[:3]:
        load.start()

    barrier = pltpu.get_barrier_semaphore()
    for i in range(1, GX):
        pl.semaphore_signal(barrier, inc=1, device_id=((gx + i) % GX, gy), device_id_type=MESH)

    @pl.loop(1, GY)
    def _(i):
        pl.semaphore_signal(barrier, inc=1, device_id=(gx, (gy + i) % GY), device_id_type=MESH)

    pl.semaphore_wait(barrier, GX + GY - 2)

    def gat(s, p, yy, cc):
        return G.at[s, p, yy, cc]

    def half(ref, i):
        return ref.at[:, pl.ds(i * (ROWS // 2), ROWS // 2)]

    def own(s, p):
        lev = pl.ds((p % 2) * PLEV, PLEV)
        src = ctrl.at[p // 2, lev] if s == 0 else F.at[p // 2, lev]
        dst = gat(s, p, y, c)
        rcopy(src, dst, xs_send.at[s, p, 0], xs_recv.at[s, p, 0], col(yp)).start()
        rcopy(src, dst, xs_send.at[s, p, 1], xs_recv.at[s, p, 1], col(ym)).start()
        rcopy(src, dst, xs_send.at[s, p, 2], xs_recv.at[s, p, 2], sib).start()
        pltpu.make_async_copy(src, dst, own_sem.at[s, p]).start()

    def near(s, p):
        for i, (yy, to) in enumerate(((ym, yp), (yp, ym))):
            piece = gat(s, p, yy, c)
            wait(piece, xs_recv.at[s, p, i])
            part = half(piece, i)
            rcopy(part, part, xs_send.at[s, p, 3 + i], xs_recv.at[s, p, 3 + i], col(to)).start()
            rcopy(piece, piece, xs_send.at[s, p, 5 + i], xs_recv.at[s, p, 5 + i], sib).start()

    def far(s, p):
        for i in range(2):
            part = half(gat(s, p, yo, c), i)
            wait(part, xs_recv.at[s, p, 3 + i])
            rcopy(part, part, xs_send.at[s, p, 7 + i], xs_recv.at[s, p, 7 + i], sib).start()

    def chunk(s, p, yy):
        lhs = jnp.concatenate([G[s, p, yy, i].reshape(PLEV * ROWS, COLS) for i in range(2)], axis=1)
        hi, lo = split2(lhs)
        rhs = XT[pl.ds(pl.multiple_of(yy * 2 * COLS, 2 * COLS), 2 * COLS), :]
        pr = jnp.dot(hi, rhs, preferred_element_type=F32)
        qr = jnp.dot(lo, rhs[:, :COLS], preferred_element_type=F32)
        return (pr[:, :COLS] + pr[:, COLS:]) + qr

    def mult_near(s, p):
        wait(gat(s, p, y, c), own_sem.at[s, p])
        wait(gat(s, p, y, 1 - c), xs_recv.at[s, p, 2])
        wait(gat(s, p, ym, 1 - c), xs_recv.at[s, p, 5])
        wait(gat(s, p, yp, 1 - c), xs_recv.at[s, p, 6])
        acc[p] = jnp.zeros((PLEV * ROWS, COLS), F32)

        @pl.loop(0, YR - 1)
        def _(t):
            acc[p] += chunk(s, p, (y + t * (t + 1) // 2) % YR)

    def mult_far(s, p):
        for i in range(2):
            wait(half(gat(s, p, yo, 1 - c), i), xs_recv.at[s, p, 7 + i])
        total = acc[p] + chunk(s, p, yo)
        k, first = p // 2, (p % 2) * PUNITS
        for lb in range(LB):
            m = sea_v[:, lb * LANES : (lb + 1) * LANES].astype(F32)
            for f in range(PLEV):
                xout[s, k, first + f * LB + lb] = (
                    m * total[f * ROWS : (f + 1) * ROWS, lb * LANES : (lb + 1) * LANES]
                )

        @pl.loop(0, PUNITS)
        def _(i):
            u = first + (i + gy) % PUNITS
            g = worker(k, u)
            src = xout.at[s, k, u]
            dst = U.at[s, k, pl.ds(pl.multiple_of(gy * ROWS, ROWS), ROWS)]

            @pl.when(g != gy)
            def _():
                rcopy(src, dst, a_send.at[s, k], a_recv.at[s, k], (gx, g)).start()

            @pl.when(g == gy)
            def _():
                pltpu.make_async_copy(src, dst, a_recv.at[s, k]).start()

    def y_load(s, k):
        @pl.when(my_unit(k) < UNITS)
        def _():
            wait(U.at[s, k], a_recv.at[s, k])
            hi, lo = split2(U[s, k])
            W[:, :LANES] = hi
            W[:, LANES:] = lo

    def y_rows(s, k, begin, end):
        unit = my_unit(k)

        @pl.when(unit < UNITS)
        def _():
            @pl.loop(begin, end)
            def _(t):
                m = (y + t * (7 - t) // 2) % YR
                rows = pl.ds(pl.multiple_of(m * 8 * ROWS, 8 * ROWS), 8 * ROWS)
                p = jnp.dot(Yhi[rows, :], W[...], preferred_element_type=F32)
                q = jnp.dot(Ylo[rows, :], W[:, :LANES], preferred_element_type=F32)
                yout[s, k, rows] = (p[:, :LANES] + p[:, LANES:]) + q

                @pl.loop(0, 8)
                def _(i):
                    g = m * 8 + (i + gy) % 8
                    src = yout.at[s, k, pl.ds(pl.multiple_of(g * ROWS, ROWS), ROWS)]
                    dst = R.at[s, k, unit]

                    @pl.when(g != gy)
                    def _():
                        rcopy(src, dst, r_send.at[s, k], r_recv.at[s, k], (gx, g)).start()

                    @pl.when(g == gy)
                    def _():
                        pltpu.make_async_copy(src, dst, r_recv.at[s, k]).start()

    def y_phase(s, k):
        y_load(s, k)
        y_rows(s, k, 0, YR)

    def solve(s, k, lb):
        sl = slice(lb * LANES, (lb + 1) * LANES)
        m = sea_v[:, sl].astype(F32)
        d = []
        for l in range(LEV):
            v = R[s, k, l * LB + lb] * m
            if l > 0:
                v = v + kap_v[l - 1, :, sl] * d[-1]
            d.append(v * rp[l, :, sl])
        u = [d[-1]]
        for l in range(LEV - 2, -1, -1):
            u.insert(0, d[l] + cs[l, :, sl] * u[0])
        return u

    def interp_rows(vals, base):
        hi, lo = split2(vals.reshape(-1, COLS))
        p = jnp.dot(hi, wx[...], preferred_element_type=F32)
        q = jnp.dot(lo, wx[:, :SLOTS], preferred_element_type=F32)
        v = ((p[:, :SLOTS] + p[:, SLOTS:]) + q).reshape(-1, ROWS, SLOTS)
        for i in range(v.shape[0]):
            ob_i[pl.ds(base + i, 1), :] = jnp.sum(v[i] * wy[...], axis=0, keepdims=True)

    def yblock(shard, xx, n=1):
        return Yf.at[pl.ds(pl.multiple_of(shard * YSH + xx * YSB, YSB), n * YSB)]

    def yhalf(shard, xx, i):
        return Yf.at[pl.ds(pl.multiple_of(shard * YSH + xx * YSB + i * (YSB // 2), YSB // 2), YSB // 2)]

    def row_dev(xx):
        return (gx, xx * NZ + z)

    def to_sib(ref, i, group):
        rcopy(ref, ref, yb_send.at[i], yb_recv.at[group], sib).start()

    def along_x(i, yy):
        block = yblock(2 * yy + c, x)
        rcopy(block, block, yx_send.at[i, 0], yx_recv.at[i, 0], row_dev(xp)).start()
        rcopy(block, block, yx_send.at[i, 1], yx_recv.at[i, 1], row_dev(xm)).start()
        to_sib(block, 1 + i, 1 + i)

    def y_near():
        for i, (yy, to) in enumerate(((ym, yp), (yp, ym))):
            block = yblock(2 * yy + c, x)
            wait(block, ys_recv.at[i])
            part = yhalf(2 * yy + c, x, i)
            rcopy(part, part, ys_send.at[2 + i], ys_recv.at[2 + i], col(to)).start()
            along_x(i, yy)

    def y_far():
        for i in range(2):
            wait(yhalf(2 * yo + c, x, i), ys_recv.at[2 + i])
        along_x(2, yo)

    def x_near(i):
        yy = (ym, yp, yo)[i]
        for j, (xx, to) in enumerate(((xm, xp), (xp, xm))):
            block = yblock(2 * yy + c, xx)
            wait(block, yx_recv.at[i, j])
            part = yhalf(2 * yy + c, xx, j)
            rcopy(part, part, yx_send.at[i, 2 + j], yx_recv.at[i, 2 + j], row_dev(to)).start()
            to_sib(block, 4 + 4 * i + j, 1 + i)

    def x_far(i):
        yy = (ym, yp, yo)[i]
        for j in range(2):
            part = yhalf(2 * yy + c, xo, j)
            wait(part, yx_recv.at[i, 2 + j])
            to_sib(part, 6 + 4 * i + j, 1 + i)

    def y_split(group):
        yy = (y, ym, yp, yo)[group]
        wait(yblock(0, 0, NX), yb_recv.at[group])

        @pl.loop(0, 2)
        def _(cc):
            rows = pl.ds(pl.multiple_of((2 * yy + cc) * YSH, YSH), YSH)
            hi, lo = split2(Yf[rows, :])
            Yhi[rows, :] = hi
            Ylo[rows, :] = lo

    def turn(lo_, hi_):
        @pl.loop(lo_, hi_)
        def _(j):
            at = pl.ds(pl.multiple_of(j * 256, 256), 256)
            hi, lo = split2(xbuf[:, at].T)
            XT[at, :COLS] = hi
            XT[at, COLS:] = lo

    xp, xm, xo = (x + 1) % NX, (x + NX - 1) % NX, (x + 2) % NX
    yrow = yinv.at[pl.ds(pl.multiple_of(x * YSB, YSB), YSB)]
    for i, yy in enumerate((yp, ym)):
        rcopy(yrow, yblock(gx, x), ys_send.at[i], ys_recv.at[i], col(yy)).start()
    own(0, 0)
    rcopy(yinv, yblock(gx, 0, NX), yb_send.at[0], yb_recv.at[0], sib).start()
    for load in loads[3:]:
        load.start()

    loads[1].wait()
    loads[2].wait()
    for lb in range(LB):
        sl = slice(lb * LANES, (lb + 1) * LANES)
        prev = None
        for l in range(LEV):
            diag = 1.0
            if l > 0:
                diag = diag + kap_v[l - 1, :, sl]
            if l < LEV - 1:
                diag = diag + kap_v[l, :, sl]
            pivot = diag if l == 0 else diag - kap_v[l - 1, :, sl] * prev
            rec = 1.0 / pivot
            rp[l, :, sl] = rec
            if l < LEV - 1:
                prev = kap_v[l, :, sl] * rec
                cs[l, :, sl] = prev

    def first_solve(k):
        wait(R.at[0, k], r_recv.at[0, k])
        for lb in range(LB):
            u = solve(0, k, lb)
            for l in range(LEV):
                F[k, l, :, lb * LANES : (lb + 1) * LANES] = u[l]

    loads[0].wait()
    turn(0, 6)
    y_near()
    own(0, 1)
    turn(6, 12)
    near(0, 0)
    own(0, 2)
    y_far()
    mult_near(0, 0)
    near(0, 1)
    own(0, 3)
    x_near(0)
    x_near(1)
    far(0, 0)
    mult_far(0, 0)
    mult_near(0, 1)
    near(0, 2)
    x_near(2)
    far(0, 1)
    mult_far(0, 1)
    mult_near(0, 2)
    near(0, 3)
    x_far(0)
    far(0, 2)
    mult_far(0, 2)
    x_far(1)
    far(0, 3)
    x_far(2)
    loads[5].wait()
    y_split(0)
    mult_near(0, 3)
    y_split(1)
    y_split(2)
    y_load(0, 0)
    y_split(3)
    y_rows(0, 0, 0, 4)
    mult_far(0, 3)

    row = tidx[...]
    three = row >> 7
    trow = (three * 171) >> 9
    tcol = row - trow * COLS
    fx, fy = frac[0:1, :], frac[1:2, :]
    lon = lax.broadcasted_iota(I32, (COLS, SLOTS), 0)
    whi, wlo = split2(jnp.where(lon == tcol, 1.0 - fx, jnp.where(lon == tcol + 1, fx, 0.0)))
    wx[:, :SLOTS] = whi
    wx[:, SLOTS:] = wlo
    lat = lax.broadcasted_iota(I32, (ROWS, SLOTS), 0)
    wy[...] = jnp.where(lat == trow, 1.0 - fy, jnp.where(lat == trow + 1, fy, 0.0))
    own_row = owner[...]
    ia = lax.broadcasted_iota(I32, (SLOTS, SLOTS), 0)
    ib = lax.broadcasted_iota(I32, (SLOTS, SLOTS), 1)
    own_f = own_row.astype(F32)
    own_col = jnp.sum(jnp.where(ia == ib, own_f, 0.0), axis=1, keepdims=True)
    earlier = jnp.where((own_col == own_f) & (ia < ib), 1.0, 0.0)
    rank = jnp.sum(earlier, axis=0, keepdims=True)
    live = lax.broadcasted_iota(I32, (1, SLOTS), 1) < count[0]
    ogx, ogy = own_row // GY, own_row % GY
    slot[0:1, :] = jnp.where(live, rank, -1.0)
    slot[1:2, :] = (ogx % 4).astype(F32)
    line = lax.broadcasted_iota(I32, (GY, SLOTS), 0)
    for h in range(2):
        picks[h] = jnp.where((line == ogy) & (ogx // 4 == h), 1.0, 0.0).astype(BF16)


    first_solve(0)
    own(1, 0)
    own(1, 1)
    y_phase(0, 1)
    near(1, 0)
    mult_near(1, 0)
    near(1, 1)
    first_solve(1)
    own(1, 2)
    own(1, 3)
    far(1, 0)
    mult_far(1, 0)
    mult_near(1, 1)
    far(1, 1)
    mult_far(1, 1)
    near(1, 2)
    mult_near(1, 2)
    near(1, 3)
    far(1, 2)
    mult_far(1, 2)
    far(1, 3)
    mult_near(1, 3)
    mult_far(1, 3)
    y_phase(1, 0)
    y_phase(1, 1)

    loads[3].wait()
    loads[4].wait()
    wait(R.at[1, 0], r_recv.at[1, 0])
    for lb in range(LB):
        sl = slice(lb * LANES, (lb + 1) * LANES)
        u = solve(1, 0, lb)
        for l in range(LEV):
            inc[0, l, :, sl] = sig_v[0, l, :, sl] * u[l]
    ob_i[...] = jnp.zeros_like(ob_i)
    interp_rows(inc[0], 0)
    wait(R.at[1, 1], r_recv.at[1, 1])
    for lb in range(LB):
        sl = slice(lb * LANES, (lb + 1) * LANES)
        u = solve(1, 1, lb)
        h = None
        for l in range(LEV):
            t = inc[0, l, :, sl]
            v = sig_v[1, l, :, sl] * u[l] + bet_v[l, :, sl] * t
            inc[1, l, :, sl] = v
            term = ssh[0, l] * t + ssh[1, l] * v
            h = term if h is None else h + term
        height[:, sl] = h
    interp_rows(inc[1], LEV)
    interp_rows(height[...], 2 * LEV)

    rank, quarter = slot[0:1, :], slot[1:2, :]
    values = ob_i[...]
    both = jnp.concatenate([jnp.where(rank == 0.0, values, 0.0), jnp.where(rank == 1.0, values, 0.0)], axis=0)
    placed = jnp.concatenate([jnp.where(quarter == q, both, 0.0) for q in range(4)], axis=0)
    hi, mid = split2(placed)
    low = ((placed - hi.astype(F32)) - mid.astype(F32)).astype(BF16)
    dims = (((1,), (1,)), ((), ()))
    for h in range(2):
        pick = picks[h]
        ob_o[:, h, :] = (
            lax.dot_general(pick, hi, dims, preferred_element_type=F32)
            + lax.dot_general(pick, mid, dims, preferred_element_type=F32)
        ) + lax.dot_general(pick, low, dims, preferred_element_type=F32)

    @pl.loop(1, GY)
    def _(i):
        g = (gy + i) % GY
        rcopy(ob_o.at[g], ob_a.at[gy], o_send.at[0], o_recv.at[0], (gx, g)).start()

    pltpu.make_async_copy(ob_o.at[gy], ob_a.at[gy], o_recv.at[0]).start()
    wait(ob_a, o_recv.at[0])
    for g in range(GX):
        part = ob_a[:, g // 4, :]
        ob_m[g] = pltpu.roll(part, (LANES - 32 * (g % 4)) % LANES, 1) if g % 4 else part
    for g in range(GX):
        src = ob_m.at[g]
        dst = ob_f.at[pl.ds(pl.multiple_of(gx * GY, GY), GY)]

        @pl.when(g != gx)
        def _():
            rcopy(src, dst, o_send.at[1], o_recv.at[1], (g, gy)).start()

        @pl.when(g == gx)
        def _():
            pltpu.make_async_copy(src, dst, o_recv.at[1]).start()

    wait(ob_f, o_recv.at[1])
    turned = ob_f[...].T
    obs[:, 0, :] = turned[0:REC]
    obs[:, 1, :] = turned[16 : 16 + REC]

    for s in range(STEPS):
        for p in range(PIECES):
            whole = gat(s, p, y, c)
            for i in range(9):
                wait(half(whole, 0) if i in (3, 4, 7, 8) else whole, xs_send.at[s, p, i])
        for k in range(KINDS):
            mine = my_unit(k) < UNITS

            @pl.when(mine)
            def _():
                wait(xout.at[s, k, pl.ds(0, UNITS - 1)], a_send.at[s, k])
                wait(yout.at[s, k, pl.ds(0, (GY - 1) * ROWS)], r_send.at[s, k])

            @pl.when(jnp.logical_not(mine))
            def _():
                wait(xout.at[s, k], a_send.at[s, k])

    for i in range(4):
        wait(yblock(0, 0) if i < 2 else yhalf(0, 0, 0), ys_send.at[i])
    for i in range(3):
        for j in range(4):
            wait(yblock(0, 0) if j < 2 else yhalf(0, 0, 0), yx_send.at[i, j])
            wait(yblock(0, 0) if j < 2 else yhalf(0, 0, 0), yb_send.at[4 + 4 * i + j])
        wait(yblock(0, 0), yb_send.at[1 + i])
    wait(yblock(0, 0, NX), yb_send.at[0])
    wait(ob_o.at[pl.ds(0, GY - 1)], o_send.at[0])
    wait(ob_m.at[pl.ds(0, GX - 1)], o_send.at[1])


def copy_out(a, b, d, oa, ob, od):
    oa[...] = a[...]
    ob[...] = b[...]
    od[...] = d[...]


def body(
    control, sigma, kappa, beta, sea_mask, x_inverse, y_inverse, ssh_coef, obs_owner, tile_index, obs_frac, obs_count
):
    vmem = pl.BlockSpec(memory_space=pltpu.VMEM)
    smem = pl.BlockSpec(memory_space=pltpu.SMEM)
    hbm = pl.BlockSpec(memory_space=ANY)
    dma = pltpu.SemaphoreType.DMA
    tile = (ROWS, COLS)
    inc, height, obs = pl.pallas_call(
        kernel,
        out_shape=(
            jax.ShapeDtypeStruct((KINDS, LEV) + tile, F32),
            jax.ShapeDtypeStruct(tile, F32),
            jax.ShapeDtypeStruct((REC, CAP, DEV), F32),
        ),
        in_specs=[hbm] * 7 + [smem, vmem, vmem, vmem, smem],
        out_specs=(vmem, vmem, vmem),
        scratch_shapes=[
            pltpu.VMEM((STEPS, PIECES, YR, 2, PLEV) + tile, F32),
            pltpu.VMEM((NLON, 2 * COLS), BF16),
            pltpu.VMEM((COLS, NLON), F32),
            pltpu.VMEM((NLAT, NLAT), F32),
            pltpu.VMEM((NLAT, NLAT), BF16),
            pltpu.VMEM((NLAT, NLAT), BF16),
            pltpu.VMEM((STEPS, KINDS, NLAT, LANES), F32),
            pltpu.VMEM((STEPS, KINDS, UNITS, ROWS, LANES), F32),
            pltpu.VMEM((STEPS, KINDS, UNITS, ROWS, LANES), F32),
            pltpu.VMEM((STEPS, KINDS, NLAT, LANES), F32),
            pltpu.VMEM((KINDS, LEV) + tile, F32),
            pltpu.VMEM((PIECES, PLEV * ROWS, COLS), F32),
            pltpu.VMEM((NLAT, 2 * LANES), BF16),
            pltpu.VMEM((LEV - 1,) + tile, F32),
            pltpu.VMEM((LEV,) + tile, F32),
            pltpu.VMEM((KINDS, LEV) + tile, F32),
            pltpu.VMEM((LEV - 1,) + tile, F32),
            pltpu.VMEM((LEV,) + tile, F32),
            pltpu.VMEM(tile, I32),
            pltpu.VMEM((COLS, 2 * SLOTS), BF16),
            pltpu.VMEM((ROWS, SLOTS), F32),
            pltpu.VMEM((8, SLOTS), F32),
            pltpu.VMEM((2, GY, SLOTS), BF16),
            pltpu.VMEM((16, SLOTS), F32),
            pltpu.VMEM((GY, 2, LANES), F32),
            pltpu.VMEM((GY, 2, LANES), F32),
            pltpu.VMEM((GX, GY, LANES), F32),
            pltpu.VMEM((DEV, LANES), F32),
            dma((STEPS, PIECES)),
            dma((6,)),
            dma((STEPS, PIECES, 9)),
            dma((STEPS, PIECES, 9)),
            dma((4,)),
            dma((4,)),
            dma((3, 4)),
            dma((3, 4)),
            dma((16,)),
            dma((4,)),
            dma((STEPS, KINDS)),
            dma((STEPS, KINDS)),
            dma((STEPS, KINDS)),
            dma((STEPS, KINDS)),
            dma((2,)),
            dma((2,)),
        ],
        compiler_params=pltpu.CompilerParams(
            collective_id=0, has_side_effects=True, vmem_limit_bytes=62 * 1024 * 1024
        ),
        name="covariance",
    )(
        control[0],
        sigma,
        kappa,
        beta,
        sea_mask,
        x_inverse,
        y_inverse,
        ssh_coef,
        obs_owner.reshape(1, SLOTS),
        tile_index.reshape(1, SLOTS),
        obs_frac,
        obs_count,
    )
    results = (inc, height, obs)
    inc, height, obs = pl.pallas_call(
        copy_out,
        out_shape=tuple(jax.ShapeDtypeStruct(r.shape, F32) for r in results),
        in_specs=[vmem] * 3,
        out_specs=(vmem,) * 3,
        name="outputs",
    )(*results)
    return inc[None], height[None], jnp.swapaxes(obs, 0, 1)


def solution(mesh):
    return jax.shard_map(
        body,
        mesh=mesh,
        in_specs=(
            P(None, None, None, "gy", "gx"),
            P(None, None, "gy", "gx"),
            P(None, "gy", "gx"),
            P(None, "gy", "gx"),
            P("gy", "gx"),
            P("gx", None),
            P("gx", None),
            P(),
            P(("gx", "gy"), None),
            P(("gx", "gy")),
            P(None, ("gx", "gy")),
            P(("gx", "gy")),
        ),
        out_specs=(
            P(None, None, None, "gy", "gx"),
            P(None, "gy", "gx"),
            P(None, None, ("gx", "gy")),
        ),
        check_vma=False,
    )
```

```python
import functools

import jax
import jax.numpy as jnp
from jax import lax
from jax.experimental import pallas as pl
from jax.experimental.pallas import tpu as pltpu
from jax.sharding import PartitionSpec as P

F32, BF16, I32 = jnp.float32, jnp.bfloat16, jnp.int32
MESH = pl.DeviceIdType.MESH
ANY = pl.ANY

STEPS, KINDS, LEV = 2, 2, 6
ROWS, COLS, LANES = 48, 384, 128
LB = COLS // LANES
UNITS = LEV * LB
YR, NX, NZ = 4, 4, 8
GX, GY = 2 * YR, NX * NZ
NLAT, NLON = GY * ROWS, GX * COLS
YSH = NLAT // GX
YSB = YSH // NX
SLOTS, CAP, REC, DEV = 256, 2, 13, GX * GY
PIECES, PLEV = 4, LEV // 2
PUNITS = PLEV * LB


def split2(v):
    hi = v.astype(BF16)
    lo = (v - hi.astype(F32)).astype(BF16)
    return hi, lo


def kernel(
    ctrl,
    sigma,
    kappa,
    beta,
    sea,
    xinv,
    yinv,
    ssh,
    owner,
    tidx,
    frac,
    count,
    inc_o,
    height_o,
    obs,
    inc,
    height,
    G,
    XT,
    xbuf,
    Yf,
    Yhi,
    Ylo,
    U,
    R,
    xout,
    yout,
    F,
    acc,
    W,
    cs,
    rp,
    sig_v,
    kap_v,
    bet_v,
    sea_v,
    wx,
    wy,
    slot,
    picks,
    ob_i,
    ob_o,
    ob_a,
    ob_m,
    ob_f,
    own_sem,
    in_sem,
    xs_send,
    xs_recv,
    ys_send,
    ys_recv,
    yx_send,
    yx_recv,
    yb_send,
    yb_recv,
    a_send,
    a_recv,
    r_send,
    r_recv,
    o_send,
    o_recv,
    out_sem,
):
    gx, gy = lax.axis_index("gx"), lax.axis_index("gy")
    y, c = gx // 2, gx % 2
    x, z = gy // NZ, gy % NZ
    yp, ym, yo = (y + 1) % YR, (y + YR - 1) % YR, (y + 2) % YR
    sib = (2 * y + 1 - c, gy)

    def col(yy):
        return (2 * yy + c, gy)

    def rcopy(src, dst, ssem, rsem, dev):
        return pltpu.make_async_remote_copy(
            src_ref=src, dst_ref=dst, send_sem=ssem, recv_sem=rsem, device_id=dev, device_id_type=MESH
        )

    def wait(ref, sem):
        pltpu.make_async_copy(ref, ref, sem).wait()

    def worker(kind, u):
        q = (18 * kind + 18 * c + u) % GY
        wx_ = q % NX
        return wx_ * NZ + (q // NX + 2 * wx_) % NZ

    def my_unit(kind):
        q = ((z + 2 * NZ - 2 * x) % NZ) * NX + x
        return (q + 4 * GY - 18 * kind - 18 * c) % GY

    loads = [
        pltpu.make_async_copy(xinv, xbuf, in_sem.at[0]),
        pltpu.make_async_copy(kappa, kap_v, in_sem.at[1]),
        pltpu.make_async_copy(sea, sea_v, in_sem.at[2]),
        pltpu.make_async_copy(sigma, sig_v, in_sem.at[3]),
        pltpu.make_async_copy(beta, bet_v, in_sem.at[4]),
        pltpu.make_async_copy(yinv, Yf.at[pl.ds(gx * YSH, YSH)], in_sem.at[5]),
    ]
    for load in loads[:3]:
        load.start()

    barrier = pltpu.get_barrier_semaphore()
    for i in range(1, GX):
        pl.semaphore_signal(barrier, inc=1, device_id=((gx + i) % GX, gy), device_id_type=MESH)

    @pl.loop(1, GY)
    def _(i):
        pl.semaphore_signal(barrier, inc=1, device_id=(gx, (gy + i) % GY), device_id_type=MESH)

    pl.semaphore_wait(barrier, GX + GY - 2)

    def gat(s, p, yy, cc):
        return G.at[s, p, yy, cc]

    def half(ref, i):
        return ref.at[:, pl.ds(i * (ROWS // 2), ROWS // 2)]

    def own(s, p):
        lev = pl.ds((p % 2) * PLEV, PLEV)
        src = ctrl.at[p // 2, lev] if s == 0 else F.at[p // 2, lev]
        dst = gat(s, p, y, c)
        rcopy(src, dst, xs_send.at[s, p, 0], xs_recv.at[s, p, 0], col(yp)).start()
        rcopy(src, dst, xs_send.at[s, p, 1], xs_recv.at[s, p, 1], col(ym)).start()
        rcopy(src, dst, xs_send.at[s, p, 2], xs_recv.at[s, p, 2], sib).start()
        pltpu.make_async_copy(src, dst, own_sem.at[s, p]).start()

    def near(s, p):
        for i, (yy, to) in enumerate(((ym, yp), (yp, ym))):
            piece = gat(s, p, yy, c)
            wait(piece, xs_recv.at[s, p, i])
            part = half(piece, i)
            rcopy(part, part, xs_send.at[s, p, 3 + i], xs_recv.at[s, p, 3 + i], col(to)).start()
            rcopy(piece, piece, xs_send.at[s, p, 5 + i], xs_recv.at[s, p, 5 + i], sib).start()

    def far(s, p):
        for i in range(2):
            part = half(gat(s, p, yo, c), i)
            wait(part, xs_recv.at[s, p, 3 + i])
            rcopy(part, part, xs_send.at[s, p, 7 + i], xs_recv.at[s, p, 7 + i], sib).start()

    def chunk(s, p, yy):
        lhs = jnp.concatenate([G[s, p, yy, i].reshape(PLEV * ROWS, COLS) for i in range(2)], axis=1)
        hi, lo = split2(lhs)
        rhs = XT[pl.ds(pl.multiple_of(yy * 2 * COLS, 2 * COLS), 2 * COLS), :]
        pr = jnp.dot(hi, rhs, preferred_element_type=F32)
        qr = jnp.dot(lo, rhs[:, :COLS], preferred_element_type=F32)
        return (pr[:, :COLS] + pr[:, COLS:]) + qr

    def mult_near(s, p):
        wait(gat(s, p, y, c), own_sem.at[s, p])
        wait(gat(s, p, y, 1 - c), xs_recv.at[s, p, 2])
        wait(gat(s, p, ym, 1 - c), xs_recv.at[s, p, 5])
        wait(gat(s, p, yp, 1 - c), xs_recv.at[s, p, 6])
        acc[p] = jnp.zeros((PLEV * ROWS, COLS), F32)

        @pl.loop(0, YR - 1)
        def _(t):
            acc[p] += chunk(s, p, (y + t * (t + 1) // 2) % YR)

    def mult_far(s, p):
        for i in range(2):
            wait(half(gat(s, p, yo, 1 - c), i), xs_recv.at[s, p, 7 + i])
        total = acc[p] + chunk(s, p, yo)
        k, first = p // 2, (p % 2) * PUNITS
        for lb in range(LB):
            m = sea_v[:, lb * LANES : (lb + 1) * LANES].astype(F32)
            for f in range(PLEV):
                xout[s, k, first + f * LB + lb] = (
                    m * total[f * ROWS : (f + 1) * ROWS, lb * LANES : (lb + 1) * LANES]
                )

        @pl.loop(0, PUNITS)
        def _(i):
            u = first + (i + gy) % PUNITS
            g = worker(k, u)
            src = xout.at[s, k, u]
            dst = U.at[s, k, pl.ds(pl.multiple_of(gy * ROWS, ROWS), ROWS)]

            @pl.when(g != gy)
            def _():
                rcopy(src, dst, a_send.at[s, k], a_recv.at[s, k], (gx, g)).start()

            @pl.when(g == gy)
            def _():
                pltpu.make_async_copy(src, dst, a_recv.at[s, k]).start()

    def y_load(s, k):
        @pl.when(my_unit(k) < UNITS)
        def _():
            wait(U.at[s, k], a_recv.at[s, k])
            hi, lo = split2(U[s, k])
            W[:, :LANES] = hi
            W[:, LANES:] = lo

    def y_rows(s, k, begin, end):
        unit = my_unit(k)

        @pl.when(unit < UNITS)
        def _():
            @pl.loop(begin, end)
            def _(t):
                m = (y + t * (7 - t) // 2) % YR
                rows = pl.ds(pl.multiple_of(m * 8 * ROWS, 8 * ROWS), 8 * ROWS)
                p = jnp.dot(Yhi[rows, :], W[...], preferred_element_type=F32)
                q = jnp.dot(Ylo[rows, :], W[:, :LANES], preferred_element_type=F32)
                yout[s, k, rows] = (p[:, :LANES] + p[:, LANES:]) + q

                @pl.loop(0, 8)
                def _(i):
                    g = m * 8 + (i + gy) % 8
                    src = yout.at[s, k, pl.ds(pl.multiple_of(g * ROWS, ROWS), ROWS)]
                    dst = R.at[s, k, unit]

                    @pl.when(g != gy)
                    def _():
                        rcopy(src, dst, r_send.at[s, k], r_recv.at[s, k], (gx, g)).start()

                    @pl.when(g == gy)
                    def _():
                        pltpu.make_async_copy(src, dst, r_recv.at[s, k]).start()

    def y_phase(s, k):
        y_load(s, k)
        y_rows(s, k, 0, YR)

    def solve(s, k, lb):
        sl = slice(lb * LANES, (lb + 1) * LANES)
        m = sea_v[:, sl].astype(F32)
        d = []
        for l in range(LEV):
            v = R[s, k, l * LB + lb] * m
            if l > 0:
                v = v + kap_v[l - 1, :, sl] * d[-1]
            d.append(v * rp[l, :, sl])
        u = [d[-1]]
        for l in range(LEV - 2, -1, -1):
            u.insert(0, d[l] + cs[l, :, sl] * u[0])
        return u

    def interp_rows(vals, base):
        hi, lo = split2(vals.reshape(-1, COLS))
        p = jnp.dot(hi, wx[...], preferred_element_type=F32)
        q = jnp.dot(lo, wx[:, :SLOTS], preferred_element_type=F32)
        v = ((p[:, :SLOTS] + p[:, SLOTS:]) + q).reshape(-1, ROWS, SLOTS)
        for i in range(v.shape[0]):
            ob_i[pl.ds(base + i, 1), :] = jnp.sum(v[i] * wy[...], axis=0, keepdims=True)

    def yblock(shard, xx, n=1):
        return Yf.at[pl.ds(pl.multiple_of(shard * YSH + xx * YSB, YSB), n * YSB)]

    def yhalf(shard, xx, i):
        return Yf.at[pl.ds(pl.multiple_of(shard * YSH + xx * YSB + i * (YSB // 2), YSB // 2), YSB // 2)]

    def row_dev(xx):
        return (gx, xx * NZ + z)

    def to_sib(ref, i, group):
        rcopy(ref, ref, yb_send.at[i], yb_recv.at[group], sib).start()

    def along_x(i, yy):
        block = yblock(2 * yy + c, x)
        rcopy(block, block, yx_send.at[i, 0], yx_recv.at[i, 0], row_dev(xp)).start()
        rcopy(block, block, yx_send.at[i, 1], yx_recv.at[i, 1], row_dev(xm)).start()
        to_sib(block, 1 + i, 1 + i)

    def y_near():
        for i, (yy, to) in enumerate(((ym, yp), (yp, ym))):
            block = yblock(2 * yy + c, x)
            wait(block, ys_recv.at[i])
            part = yhalf(2 * yy + c, x, i)
            rcopy(part, part, ys_send.at[2 + i], ys_recv.at[2 + i], col(to)).start()
            along_x(i, yy)

    def y_far():
        for i in range(2):
            wait(yhalf(2 * yo + c, x, i), ys_recv.at[2 + i])
        along_x(2, yo)

    def x_near(i):
        yy = (ym, yp, yo)[i]
        for j, (xx, to) in enumerate(((xm, xp), (xp, xm))):
            block = yblock(2 * yy + c, xx)
            wait(block, yx_recv.at[i, j])
            part = yhalf(2 * yy + c, xx, j)
            rcopy(part, part, yx_send.at[i, 2 + j], yx_recv.at[i, 2 + j], row_dev(to)).start()
            to_sib(block, 4 + 4 * i + j, 1 + i)

    def x_far(i):
        yy = (ym, yp, yo)[i]
        for j in range(2):
            part = yhalf(2 * yy + c, xo, j)
            wait(part, yx_recv.at[i, 2 + j])
            to_sib(part, 6 + 4 * i + j, 1 + i)

    def y_split(group):
        yy = (y, ym, yp, yo)[group]
        wait(yblock(0, 0, NX), yb_recv.at[group])

        @pl.loop(0, 2)
        def _(cc):
            rows = pl.ds(pl.multiple_of((2 * yy + cc) * YSH, YSH), YSH)
            hi, lo = split2(Yf[rows, :])
            Yhi[rows, :] = hi
            Ylo[rows, :] = lo

    def turn(lo_, hi_):
        @pl.loop(lo_, hi_)
        def _(j):
            at = pl.ds(pl.multiple_of(j * 256, 256), 256)
            hi, lo = split2(xbuf[:, at].T)
            XT[at, :COLS] = hi
            XT[at, COLS:] = lo

    xp, xm, xo = (x + 1) % NX, (x + NX - 1) % NX, (x + 2) % NX
    yrow = yinv.at[pl.ds(pl.multiple_of(x * YSB, YSB), YSB)]
    for i, yy in enumerate((yp, ym)):
        rcopy(yrow, yblock(gx, x), ys_send.at[i], ys_recv.at[i], col(yy)).start()
    own(0, 0)
    rcopy(yinv, yblock(gx, 0, NX), yb_send.at[0], yb_recv.at[0], sib).start()
    for load in loads[3:]:
        load.start()

    loads[1].wait()
    loads[2].wait()
    for lb in range(LB):
        sl = slice(lb * LANES, (lb + 1) * LANES)
        prev = None
        for l in range(LEV):
            diag = 1.0
            if l > 0:
                diag = diag + kap_v[l - 1, :, sl]
            if l < LEV - 1:
                diag = diag + kap_v[l, :, sl]
            pivot = diag if l == 0 else diag - kap_v[l - 1, :, sl] * prev
            rec = 1.0 / pivot
            rp[l, :, sl] = rec
            if l < LEV - 1:
                prev = kap_v[l, :, sl] * rec
                cs[l, :, sl] = prev

    def first_solve(k):
        wait(R.at[0, k], r_recv.at[0, k])
        for lb in range(LB):
            u = solve(0, k, lb)
            for l in range(LEV):
                F[k, l, :, lb * LANES : (lb + 1) * LANES] = u[l]

    loads[0].wait()
    turn(0, 6)
    y_near()
    own(0, 1)
    turn(6, 12)
    near(0, 0)
    own(0, 2)
    y_far()
    mult_near(0, 0)
    near(0, 1)
    own(0, 3)
    x_near(0)
    x_near(1)
    far(0, 0)
    mult_far(0, 0)
    mult_near(0, 1)
    near(0, 2)
    x_near(2)
    far(0, 1)
    mult_far(0, 1)
    mult_near(0, 2)
    near(0, 3)
    x_far(0)
    far(0, 2)
    mult_far(0, 2)
    x_far(1)
    far(0, 3)
    x_far(2)
    loads[5].wait()
    y_split(0)
    mult_near(0, 3)
    y_split(1)
    y_split(2)
    y_load(0, 0)
    y_split(3)
    y_rows(0, 0, 0, 4)
    mult_far(0, 3)

    row = tidx[...]
    three = row >> 7
    trow = (three * 171) >> 9
    tcol = row - trow * COLS
    fx, fy = frac[0:1, :], frac[1:2, :]
    lon = lax.broadcasted_iota(I32, (COLS, SLOTS), 0)
    whi, wlo = split2(jnp.where(lon == tcol, 1.0 - fx, jnp.where(lon == tcol + 1, fx, 0.0)))
    wx[:, :SLOTS] = whi
    wx[:, SLOTS:] = wlo
    lat = lax.broadcasted_iota(I32, (ROWS, SLOTS), 0)
    wy[...] = jnp.where(lat == trow, 1.0 - fy, jnp.where(lat == trow + 1, fy, 0.0))
    own_row = owner[...]
    ia = lax.broadcasted_iota(I32, (SLOTS, SLOTS), 0)
    ib = lax.broadcasted_iota(I32, (SLOTS, SLOTS), 1)
    own_f = own_row.astype(F32)
    own_col = jnp.sum(jnp.where(ia == ib, own_f, 0.0), axis=1, keepdims=True)
    earlier = jnp.where((own_col == own_f) & (ia < ib), 1.0, 0.0)
    rank = jnp.sum(earlier, axis=0, keepdims=True)
    live = lax.broadcasted_iota(I32, (1, SLOTS), 1) < count[0]
    ogx, ogy = own_row // GY, own_row % GY
    slot[0:1, :] = jnp.where(live, rank, -1.0)
    slot[1:2, :] = (ogx % 4).astype(F32)
    line = lax.broadcasted_iota(I32, (GY, SLOTS), 0)
    for h in range(2):
        picks[h] = jnp.where((line == ogy) & (ogx // 4 == h), 1.0, 0.0).astype(BF16)


    first_solve(0)
    own(1, 0)
    own(1, 1)
    y_phase(0, 1)
    near(1, 0)
    mult_near(1, 0)
    near(1, 1)
    first_solve(1)
    own(1, 2)
    own(1, 3)
    far(1, 0)
    mult_far(1, 0)
    mult_near(1, 1)
    far(1, 1)
    mult_far(1, 1)
    near(1, 2)
    mult_near(1, 2)
    near(1, 3)
    far(1, 2)
    mult_far(1, 2)
    far(1, 3)
    mult_near(1, 3)
    mult_far(1, 3)
    y_phase(1, 0)
    y_phase(1, 1)

    loads[3].wait()
    loads[4].wait()
    wait(R.at[1, 0], r_recv.at[1, 0])
    for lb in range(LB):
        sl = slice(lb * LANES, (lb + 1) * LANES)
        u = solve(1, 0, lb)
        for l in range(LEV):
            inc[0, l, :, sl] = sig_v[0, l, :, sl] * u[l]
    ob_i[...] = jnp.zeros_like(ob_i)
    interp_rows(inc[0], 0)
    wait(R.at[1, 1], r_recv.at[1, 1])
    for lb in range(LB):
        sl = slice(lb * LANES, (lb + 1) * LANES)
        u = solve(1, 1, lb)
        h = None
        for l in range(LEV):
            t = inc[0, l, :, sl]
            v = sig_v[1, l, :, sl] * u[l] + bet_v[l, :, sl] * t
            inc[1, l, :, sl] = v
            term = ssh[0, l] * t + ssh[1, l] * v
            h = term if h is None else h + term
        height[:, sl] = h
    writes = [
        pltpu.make_async_copy(inc, inc_o, out_sem.at[0]),
        pltpu.make_async_copy(height, height_o, out_sem.at[1]),
    ]
    for write in writes:
        write.start()
    interp_rows(inc[1], LEV)
    interp_rows(height[...], 2 * LEV)

    rank, quarter = slot[0:1, :], slot[1:2, :]
    values = ob_i[...]
    both = jnp.concatenate([jnp.where(rank == 0.0, values, 0.0), jnp.where(rank == 1.0, values, 0.0)], axis=0)
    placed = jnp.concatenate([jnp.where(quarter == q, both, 0.0) for q in range(4)], axis=0)
    hi, mid = split2(placed)
    low = ((placed - hi.astype(F32)) - mid.astype(F32)).astype(BF16)
    dims = (((1,), (1,)), ((), ()))
    for h in range(2):
        pick = picks[h]
        ob_o[:, h, :] = (
            lax.dot_general(pick, hi, dims, preferred_element_type=F32)
            + lax.dot_general(pick, mid, dims, preferred_element_type=F32)
        ) + lax.dot_general(pick, low, dims, preferred_element_type=F32)

    @pl.loop(1, GY)
    def _(i):
        g = (gy + i) % GY
        rcopy(ob_o.at[g], ob_a.at[gy], o_send.at[0], o_recv.at[0], (gx, g)).start()

    pltpu.make_async_copy(ob_o.at[gy], ob_a.at[gy], o_recv.at[0]).start()
    wait(ob_a, o_recv.at[0])
    for g in range(GX):
        part = ob_a[:, g // 4, :]
        ob_m[g] = pltpu.roll(part, (LANES - 32 * (g % 4)) % LANES, 1) if g % 4 else part
        src = ob_m.at[g]
        dst = ob_f.at[pl.ds(pl.multiple_of(gx * GY, GY), GY)]

        @pl.when(g != gx)
        def _():
            rcopy(src, dst, o_send.at[1], o_recv.at[1], (g, gy)).start()

        @pl.when(g == gx)
        def _():
            pltpu.make_async_copy(src, dst, o_recv.at[1]).start()

    wait(ob_f, o_recv.at[1])
    turned = ob_f[...].T
    obs[:, 0, :] = turned[0:REC]
    obs[:, 1, :] = turned[16 : 16 + REC]

    for write in writes:
        write.wait()
    for s in range(STEPS):
        for p in range(PIECES):
            whole = gat(s, p, y, c)
            for i in range(9):
                wait(half(whole, 0) if i in (3, 4, 7, 8) else whole, xs_send.at[s, p, i])
        for k in range(KINDS):
            mine = my_unit(k) < UNITS

            @pl.when(mine)
            def _():
                wait(xout.at[s, k, pl.ds(0, UNITS - 1)], a_send.at[s, k])
                wait(yout.at[s, k, pl.ds(0, (GY - 1) * ROWS)], r_send.at[s, k])

            @pl.when(jnp.logical_not(mine))
            def _():
                wait(xout.at[s, k], a_send.at[s, k])

    for i in range(4):
        wait(yblock(0, 0) if i < 2 else yhalf(0, 0, 0), ys_send.at[i])
    for i in range(3):
        for j in range(4):
            wait(yblock(0, 0) if j < 2 else yhalf(0, 0, 0), yx_send.at[i, j])
            wait(yblock(0, 0) if j < 2 else yhalf(0, 0, 0), yb_send.at[4 + 4 * i + j])
        wait(yblock(0, 0), yb_send.at[1 + i])
    wait(yblock(0, 0, NX), yb_send.at[0])
    wait(ob_o.at[pl.ds(0, GY - 1)], o_send.at[0])
    wait(ob_m.at[pl.ds(0, GX - 1)], o_send.at[1])


def copy_out(a, b, d, oa, ob, od):
    oa[...] = a[...]
    ob[...] = b[...]
    od[...] = d[...]


def body(
    control, sigma, kappa, beta, sea_mask, x_inverse, y_inverse, ssh_coef, obs_owner, tile_index, obs_frac, obs_count
):
    vmem = pl.BlockSpec(memory_space=pltpu.VMEM)
    smem = pl.BlockSpec(memory_space=pltpu.SMEM)
    hbm = pl.BlockSpec(memory_space=ANY)
    dma = pltpu.SemaphoreType.DMA
    tile = (ROWS, COLS)
    inc, height, obs = pl.pallas_call(
        kernel,
        out_shape=(
            jax.ShapeDtypeStruct((KINDS, LEV) + tile, F32),
            jax.ShapeDtypeStruct(tile, F32),
            jax.ShapeDtypeStruct((REC, CAP, DEV), F32),
        ),
        in_specs=[hbm] * 7 + [smem, vmem, vmem, vmem, smem],
        out_specs=(hbm, hbm, vmem),
        scratch_shapes=[
            pltpu.VMEM((KINDS, LEV) + tile, F32),
            pltpu.VMEM(tile, F32),
            pltpu.VMEM((STEPS, PIECES, YR, 2, PLEV) + tile, F32),
            pltpu.VMEM((NLON, 2 * COLS), BF16),
            pltpu.VMEM((COLS, NLON), F32),
            pltpu.VMEM((NLAT, NLAT), F32),
            pltpu.VMEM((NLAT, NLAT), BF16),
            pltpu.VMEM((NLAT, NLAT), BF16),
            pltpu.VMEM((STEPS, KINDS, NLAT, LANES), F32),
            pltpu.VMEM((STEPS, KINDS, UNITS, ROWS, LANES), F32),
            pltpu.VMEM((STEPS, KINDS, UNITS, ROWS, LANES), F32),
            pltpu.VMEM((STEPS, KINDS, NLAT, LANES), F32),
            pltpu.VMEM((KINDS, LEV) + tile, F32),
            pltpu.VMEM((PIECES, PLEV * ROWS, COLS), F32),
            pltpu.VMEM((NLAT, 2 * LANES), BF16),
            pltpu.VMEM((LEV - 1,) + tile, F32),
            pltpu.VMEM((LEV,) + tile, F32),
            pltpu.VMEM((KINDS, LEV) + tile, F32),
            pltpu.VMEM((LEV - 1,) + tile, F32),
            pltpu.VMEM((LEV,) + tile, F32),
            pltpu.VMEM(tile, I32),
            pltpu.VMEM((COLS, 2 * SLOTS), BF16),
            pltpu.VMEM((ROWS, SLOTS), F32),
            pltpu.VMEM((8, SLOTS), F32),
            pltpu.VMEM((2, GY, SLOTS), BF16),
            pltpu.VMEM((16, SLOTS), F32),
            pltpu.VMEM((GY, 2, LANES), F32),
            pltpu.VMEM((GY, 2, LANES), F32),
            pltpu.VMEM((GX, GY, LANES), F32),
            pltpu.VMEM((DEV, LANES), F32),
            dma((STEPS, PIECES)),
            dma((6,)),
            dma((STEPS, PIECES, 9)),
            dma((STEPS, PIECES, 9)),
            dma((4,)),
            dma((4,)),
            dma((3, 4)),
            dma((3, 4)),
            dma((16,)),
            dma((4,)),
            dma((STEPS, KINDS)),
            dma((STEPS, KINDS)),
            dma((STEPS, KINDS)),
            dma((STEPS, KINDS)),
            dma((2,)),
            dma((2,)),
            dma((2,)),
        ],
        compiler_params=pltpu.CompilerParams(
            collective_id=0, has_side_effects=True, vmem_limit_bytes=62 * 1024 * 1024
        ),
        name="covariance",
    )(
        control[0],
        sigma,
        kappa,
        beta,
        sea_mask,
        x_inverse,
        y_inverse,
        ssh_coef,
        obs_owner.reshape(1, SLOTS),
        tile_index.reshape(1, SLOTS),
        obs_frac,
        obs_count,
    )
    results = (inc, height, obs)
    inc, height, obs = pl.pallas_call(
        copy_out,
        out_shape=tuple(jax.ShapeDtypeStruct(r.shape, F32) for r in results),
        in_specs=[vmem] * 3,
        out_specs=(vmem,) * 3,
        name="outputs",
    )(*results)
    return inc[None], height[None], jnp.swapaxes(obs, 0, 1)


def solution(mesh):
    return jax.shard_map(
        body,
        mesh=mesh,
        in_specs=(
            P(None, None, None, "gy", "gx"),
            P(None, None, "gy", "gx"),
            P(None, "gy", "gx"),
            P(None, "gy", "gx"),
            P("gy", "gx"),
            P("gx", None),
            P("gx", None),
            P(),
            P(("gx", "gy"), None),
            P(("gx", "gy")),
            P(None, ("gx", "gy")),
            P(("gx", "gy")),
        ),
        out_specs=(
            P(None, None, None, "gy", "gx"),
            P(None, "gy", "gx"),
            P(None, None, ("gx", "gy")),
        ),
        check_vma=False,
    )
```
